512 devices in a mesh: ha: 128 (over z, x, core), ta: 4 (over y).
Axes of the slice: x: 4, y: 4, z: 16, core: 2. Of those that a mesh axis runs over, the one named last changes fastest.
Arguments:
- ref_feats: bfloat16 [32, 128, 512], P(None, None, 'ta'), may hold values from -16 to 16
- crops: bfloat16 [128, 32, 160, 512], P('ha', None, None, 'ta'), may hold values from -6 to 6
- owner: int32 [2], replicated, may hold values from 0 to 127
- offsets: int32 [2, 256], replicated, may hold values from 0 to 28
- bands: int32 [2, 256], replicated, may hold values from 1 to 4
- taps: float32 [2, 256, 4], replicated, may hold values from 0.2 to 1
- filt: float32 [8, 3, 3], replicated, may hold values from -2.8 to 5.3
Outputs:
- depth: float32 [128, 512], P('ha', 'ta')
The draws below stay inside these ranges and needn't reach their ends.
All inputs are finite; a program needn't handle non-finite values.
Results may differ from the reference program's by a relative error of at most 0.0067.
Values may be sent and summed in bfloat16 or wider, within the bound.
No kernel may reach another device: no remote copies, remote signals or barrier semaphores. Data moves between devices by JAX's collectives and lax.ppermute only.
A program may use at most 64 MiB of HBM per device.

```python
import jax
import jax.numpy as jnp
from jax import lax

C = 32
G = 8
D = 256
H = 128
STEPS = 2
OFFMAX = 28
BMAX = 4
HS = 160
W = 512
N_HA = 128


def draw_ref_feats(key, part):
    first = jax.random.fold_in(jax.random.fold_in(key, 11), 0)
    base = jnp.clip(jax.random.normal(first, (C, H, W), jnp.float32), -6.0, 6.0)
    return base.astype(jnp.bfloat16)


def draw_crops(key, part):
    inner = jax.random.fold_in(key, 13)
    base = jnp.clip(jax.random.normal(inner, (N_HA, C, HS, W), jnp.float32), -6.0, 6.0)
    return base.astype(jnp.bfloat16)


def draw_filt(key, part):
    noise = jnp.clip(0.7 * jax.random.normal(jax.random.fold_in(key, 17), (G, 3, 3), jnp.float32), -2.8, 2.8)
    center = jax.random.uniform(jax.random.fold_in(key, 19), (G, 1, 1), jnp.float32, 1.5, 2.5)
    lag_rows = jnp.arange(3)[:, None]
    lag_cols = jnp.arange(3)[None, :]
    middle = jnp.logical_and(lag_rows == 1, lag_cols == 1)[None]
    return (noise + jnp.where(middle, center, 0.0)).astype(jnp.float32)


def with_ends(drawn, own_key, low, top_value):
    index_at = [jax.random.randint(jax.random.fold_in(own_key, axis), (), 0, length) for axis, length in enumerate(drawn.shape)]
    longest = drawn.shape.index(max(drawn.shape))
    neighbour = index_at[:longest] + [(index_at[longest] + 1) % drawn.shape[longest]] + index_at[longest + 1:]
    return drawn.at[tuple(index_at)].set(low).at[tuple(neighbour)].set(top_value)


def setup_inputs(seed: int = 0) -> dict:
    key_list = jax.random.split(jax.random.key(seed), 8)
    ref_feats = draw_ref_feats(jax.random.fold_in(key_list[7], 71), 0)
    crops = draw_crops(jax.random.fold_in(key_list[7], 71), 0)
    owner = jax.random.randint(key_list[2], (STEPS,), 0, N_HA).astype(jnp.int32)
    offsets = with_ends(jax.random.randint(key_list[3], (STEPS, D), 0, OFFMAX + 1), jax.random.fold_in(key_list[3], 1), 0, OFFMAX).astype(jnp.int32)
    bands = with_ends(jax.random.randint(key_list[4], (STEPS, D), 1, BMAX + 1), jax.random.fold_in(key_list[4], 1), 1, BMAX).astype(jnp.int32)
    taps = jnp.clip(jax.random.uniform(key_list[5], (STEPS, D, BMAX), jnp.float32, 0.2, 1.0), 0.2, 1.0)
    filt = draw_filt(jax.random.fold_in(key_list[7], 71), 0)
    return {"ref_feats": ref_feats, "crops": crops, "owner": owner, "offsets": offsets, "bands": bands, "taps": taps, "filt": filt}


def plane_corr(ref_feats, crop, shift_rows, band_width, tap_row):
    active = jnp.arange(tap_row.shape[0]) < band_width
    weights = jnp.where(active, tap_row, 0.0)
    weights = weights / jnp.sum(weights)
    channels, rows, cols = ref_feats.shape
    warped = jnp.zeros((channels, rows, cols), jnp.float32)
    for tap_index in range(tap_row.shape[0]):
        window = lax.dynamic_slice_in_dim(crop, (shift_rows + tap_index).astype(jnp.int32), rows, 1)
        warped = warped + weights[tap_index] * window.astype(jnp.float32)
    product = ref_feats.astype(jnp.float32) * warped
    grouped = product.reshape(G, channels // G, rows, cols)
    return jnp.sum(grouped, axis=1) / (channels // G)


def plane_cost(padded, filt, count, cols):
    cost = jnp.zeros((count, padded.shape[2], cols), jnp.float32)
    for plane_lag in range(3):
        for column_lag in range(3):
            slab = padded[plane_lag:plane_lag + count, :, :, column_lag:column_lag + cols].astype(jnp.float32)
            cost = cost + jnp.sum(slab * filt[:, plane_lag, column_lag][None, :, None, None], axis=1)
    return cost


def reference(ref_feats, crops, owner, offsets, bands, taps, filt):
    def one_plane(plane):
        total = jnp.zeros((G, H, W), jnp.float32)
        for view in range(STEPS):
            crop = crops[owner[view]]
            total = total + plane_corr(ref_feats, crop, offsets[view, plane], bands[view, plane], taps[view, plane])
        return (total / STEPS).astype(jnp.bfloat16)

    volume = lax.map(one_plane, jnp.arange(D, dtype=jnp.int32))
    padded = jnp.pad(volume, ((1, 1), (0, 0), (0, 0), (1, 1)))

    def one_cost(plane):
        slab = lax.dynamic_slice_in_dim(padded, plane, 3, 0)
        return plane_cost(slab, filt, 1, W)[0]

    costs = lax.map(one_cost, jnp.arange(D, dtype=jnp.int32))
    probs = jax.nn.softmax(costs, axis=0)
    heights = jnp.arange(D).astype(jnp.float32) / (D - 1)
    return jnp.sum(probs * heights[:, None, None], axis=0)
```

```python
import jax
import jax.numpy as jnp
from jax import lax
from jax.experimental import pallas as pl
from jax.experimental.pallas import tpu as pltpu
from jax.sharding import Mesh, PartitionSpec as P

G = 8
CG = 4
D = 256
ZH, ZL, NX, NC = 4, 4, 4, 2
SPAN = 32


def arrange(meta, first, second, out, rows):
    for view, source in enumerate((first, second)):
        for chan in range(CG):
            rows[...] = source[0, chan].astype(jnp.float32)
            for block in range(ZH):
                for phase in range(ZL):
                    picked = rows[pl.ds(SPAN * block + phase, 16, stride=ZL), :]
                    out[block * ZL + phase, view, chan] = picked.astype(jnp.bfloat16)


def arrange_call(meta, arrived):
    spec = pl.BlockSpec((1, CG, 160, 128), lambda i, m: (m[0], 0, 0, 0))
    spec_b = pl.BlockSpec((1, CG, 160, 128), lambda i, m: (m[1], 0, 0, 0))
    return pl.pallas_call(
        arrange,
        grid_spec=pltpu.PrefetchScalarGridSpec(
            num_scalar_prefetch=1,
            grid=(1,),
            in_specs=[spec, spec_b],
            out_specs=pl.BlockSpec((16, 2, CG, 16, 128), lambda i, m: (0, 0, 0, 0, 0)),
            scratch_shapes=[pltpu.VMEM((160, 128), jnp.float32)],
        ),
        out_shape=jax.ShapeDtypeStruct((16, 2, CG, 16, 128), jnp.bfloat16),
        name="arrange",
    )(meta, arrived, arrived)


def products(meta, first, second, ref, out, rows, refs):
    phase = meta[5]
    for view, source in enumerate((first, second)):
        for chan in range(CG):
            rows[view, chan] = source[0, 0, chan].astype(jnp.float32)
    for chan in range(CG):
        refs[chan] = ref[chan].astype(jnp.float32)
    for row in range(SPAN):
        start = row // ZL + jnp.where(row % ZL > phase, 1, 0)
        for view in range(2):
            total = jnp.zeros((8, 128), jnp.float32)
            for chan in range(CG):
                line = refs[chan, row : row + 1, :]
                total = total + line * rows[view, chan, pl.ds(start, 8), :]
            out[row, view] = total


def products_call(meta, arrived, ref):
    def spec(view):
        return pl.BlockSpec((1, 1, CG, 16, 128), lambda i, m: (m[2 + view], view, 0, 0, 0))

    return pl.pallas_call(
        products,
        grid_spec=pltpu.PrefetchScalarGridSpec(
            num_scalar_prefetch=1,
            grid=(1,),
            in_specs=[
                spec(0),
                spec(1),
                pl.BlockSpec((CG, SPAN, 128), lambda i, m: (m[6], m[4], 0)),
            ],
            out_specs=pl.BlockSpec((SPAN, 2, 8, 128), lambda i, m: (0, 0, 0, 0)),
            scratch_shapes=[
                pltpu.VMEM((2, CG, 16, 128), jnp.float32),
                pltpu.VMEM((CG, SPAN, 128), jnp.float32),
            ],
        ),
        out_shape=jax.ShapeDtypeStruct((SPAN, 2, 8, 128), jnp.float32),
        name="products",
    )(meta, arrived, arrived, ref)


def weigh(meta, offsets, bands, taps, out):
    sub = lax.broadcasted_iota(jnp.int32, (128, D), 0)
    packed = jnp.zeros((128, D), jnp.float32)
    for view in range(2):
        packed = jnp.where(sub == view, offsets[view : view + 1, :].astype(jnp.float32), packed)
        packed = jnp.where(sub == 2 + view, bands[view : view + 1, :].astype(jnp.float32), packed)
    packed = packed.T
    lane = lax.broadcasted_iota(jnp.int32, (D, 128), 1)
    shift = jnp.bitwise_and(lane // 16 + 4 - jnp.bitwise_and(meta[6], 3), 3)
    reach = (shift + 4 * jnp.bitwise_and(lane, 7)).astype(jnp.float32)
    side = jnp.bitwise_and(lane // 8, 1)
    total = jnp.zeros((D, 128), jnp.float32)
    for view in range(2):
        offset = packed[:, view : view + 1]
        band = packed[:, 2 + view : 3 + view]
        kept = [jnp.where(band > k, taps[view, :, k : k + 1], 0.0) for k in range(4)]
        whole = kept[0] + kept[1] + kept[2] + kept[3]
        lag = jnp.where(side == view, reach, -1.0) - offset
        for k in range(4):
            total = jnp.where(lag == k, kept[k] / whole, total)
    high = total.astype(jnp.bfloat16)
    out[:, :128] = high
    out[:, 128:] = (total - high.astype(jnp.float32)).astype(jnp.bfloat16)


def weigh_call(meta, offsets, bands, taps):
    return pl.pallas_call(
        weigh,
        grid_spec=pltpu.PrefetchScalarGridSpec(
            num_scalar_prefetch=1,
            grid=(1,),
            in_specs=[
                pl.BlockSpec((2, D), lambda i, m: (0, 0)),
                pl.BlockSpec((2, D), lambda i, m: (0, 0)),
                pl.BlockSpec((2, D, 4), lambda i, m: (0, 0, 0)),
            ],
            out_specs=pl.BlockSpec((D, 256), lambda i, m: (0, 0)),
        ),
        out_shape=jax.ShapeDtypeStruct((D, 256), jnp.bfloat16),
        name="weigh",
    )(meta, offsets, bands, taps)


def filtered(filt, weights, pieces, cost, right, left, stack, volume, sums):
    for group in range(G):
        lanes = slice(128 * group, 128 * group + 128)
        for block in range(ZL):
            piece = pieces[block * G + group].reshape(16, 128)
            high = piece.astype(jnp.bfloat16)
            low = (piece - high.astype(jnp.float32)).astype(jnp.bfloat16)
            for copy in range(2):
                at = 128 * copy + 16 * block
                stack[at : at + 16, lanes] = high
                stack[at + 64 : at + 80, lanes] = low
    volume[...] = jnp.dot(weights[...], stack[...], preferred_element_type=jnp.float32)
    zero = jnp.zeros((8, 128), jnp.float32)
    for i in range(3):
        for j in range(3):
            sums[i, j, 0:8, :] = zero
            sums[i, j, D + 8 : D + 16, :] = zero
    step = 32

    def strip(index, carry):
        at = pl.multiple_of(index * step, step)
        totals = [[jnp.zeros((step, 128), jnp.float32) for _ in range(3)] for _ in range(3)]
        for group in range(G):
            part = volume[pl.ds(at, step), 128 * group : 128 * group + 128] * 0.125
            part = part.astype(jnp.bfloat16).astype(jnp.float32)
            for i in range(3):
                for j in range(3):
                    totals[i][j] = totals[i][j] + filt[group * 9 + i * 3 + j] * part
        for i in range(3):
            for j in range(3):
                sums[i, j, pl.ds(at + 8, step), :] = totals[i][j]
        return carry

    lax.fori_loop(0, D // step, strip, 0)
    lane = lax.broadcasted_iota(jnp.int32, (D, 128), 1)
    column = [sums[0, j, 7 : D + 7, :] + sums[1, j, 8 : D + 8, :] + sums[2, j, 9 : D + 9, :] for j in range(3)]
    before = pltpu.roll(column[0], 1, 1)
    after = pltpu.roll(column[2], 127, 1)
    cost[...] = column[1] + jnp.where(lane == 0, 0.0, before) + jnp.where(lane == 127, 0.0, after)
    edges = jnp.where(lane == 0, before, after).T
    right[...] = edges[0:1, :]
    left[...] = edges[127:128, :]


def filtered_call(filt, weights, pieces):
    edge = jax.ShapeDtypeStruct((1, D), jnp.float32)
    return pl.pallas_call(
        filtered,
        in_specs=[
            pl.BlockSpec(memory_space=pltpu.SMEM),
            pl.BlockSpec(memory_space=pltpu.VMEM),
            pl.BlockSpec(memory_space=pltpu.VMEM),
        ],
        out_shape=[jax.ShapeDtypeStruct((D, 128), jnp.float32), edge, edge],
        scratch_shapes=[
            pltpu.VMEM((256, 1024), jnp.bfloat16),
            pltpu.VMEM((D, 1024), jnp.float32),
            pltpu.VMEM((3, 3, D + 16, 128), jnp.float32),
        ],
        name="filtered",
    )(filt, weights, pieces)


def expected(cost, from_left, from_right, out):
    sub = lax.broadcasted_iota(jnp.int32, (128, D), 0)
    edges = jnp.where(sub == 0, from_left[...], jnp.where(sub == 127, from_right[...], 0.0)).T
    whole = cost[...] + edges
    top = jnp.max(whole, axis=0, keepdims=True)
    grown = jnp.exp(whole - top)
    heights = lax.broadcasted_iota(jnp.int32, (D, 128), 0).astype(jnp.float32) * (1.0 / (D - 1))
    out[...] = jnp.sum(grown * heights, axis=0, keepdims=True) / jnp.sum(grown, axis=0, keepdims=True)


def expected_call(cost, from_left, from_right):
    return pl.pallas_call(
        expected,
        out_shape=jax.ShapeDtypeStruct((1, 128), jnp.float32),
        name="expected",
    )(cost, from_left, from_right)


def body(ref_feats, crops, owner, offsets, bands, taps, filt):
    block = lax.axis_index("zh")
    phase = lax.axis_index("zl")
    group = lax.axis_index("x") * NC + lax.axis_index("c")
    near = owner % G
    far = owner // G
    meta = jnp.stack([near[0], near[1], far[0], far[1], block, phase, group]).astype(jnp.int32)
    arrived = lax.all_to_all(crops[0], ("x", "c"), 0, 0, tiled=True)
    weights = weigh_call(meta, offsets, bands, taps)
    windows = arrange_call(meta, arrived.reshape(G, CG, 160, 128))
    windows = lax.all_to_all(windows, ("zh", "zl"), 0, 0, tiled=True)
    pieces = products_call(meta, windows, ref_feats)
    pieces = lax.all_to_all(pieces, ("zl", "x", "c"), 0, 0, tiled=True)
    cost, right, left = filtered_call(filt.reshape(G * 9), weights, pieces)
    count = lax.axis_size("ta")
    from_left = lax.ppermute(right, "ta", [(i, i + 1) for i in range(count - 1)])
    from_right = lax.ppermute(left, "ta", [(i + 1, i) for i in range(count - 1)])
    return expected_call(cost, from_left, from_right)


def solution(mesh):
    rows = ("zh", "zl", "x", "c")
    inner = Mesh(mesh.devices.reshape(ZH, ZL, NX, NC, mesh.shape["ta"]), rows + ("ta",))
    placed = (P(None, None, "ta"), P(rows, None, None, "ta"), P(), P(), P(), P(), P())
    return jax.shard_map(body, mesh=inner, in_specs=placed, out_specs=P(rows, "ta"), check_vma=False)
```

```python
import jax
import jax.numpy as jnp
from jax import lax
from jax.experimental import pallas as pl
from jax.experimental.pallas import tpu as pltpu
from jax.sharding import Mesh, PartitionSpec as P

G = 8
CG = 4
D = 256
ZH, ZL, NX, NC = 4, 4, 4, 2
SPAN = 32


def arrange(meta, *refs):
    *sources, out, rows = refs
    for view, source in enumerate(sources):
        for chan in range(CG):
            rows[...] = source[0, chan].astype(jnp.float32)
            for block in range(ZH):
                for phase in range(ZL):
                    picked = rows[pl.ds(SPAN * block + phase, 16, stride=ZL), :]
                    out[block * ZL + phase, view, chan] = picked.astype(jnp.bfloat16)


def arrange_call(meta, arrived, picks):
    def spec(pick):
        return pl.BlockSpec((1, CG, 160, 128), lambda i, m: (m[pick], 0, 0, 0))

    shape = (16, len(picks), CG, 16, 128)
    return pl.pallas_call(
        arrange,
        grid_spec=pltpu.PrefetchScalarGridSpec(
            num_scalar_prefetch=1,
            grid=(1,),
            in_specs=[spec(pick) for pick in picks],
            out_specs=pl.BlockSpec(shape, lambda i, m: (0, 0, 0, 0, 0)),
            scratch_shapes=[pltpu.VMEM((160, 128), jnp.float32)],
        ),
        out_shape=jax.ShapeDtypeStruct(shape, jnp.bfloat16),
        name="arrange",
    )(meta, *[arrived] * len(picks))


def products(meta, first, second, ref, out, rows, refs):
    phase = meta[5]
    for view, source in enumerate((first, second)):
        for chan in range(CG):
            rows[view, chan] = source[0, 0, chan].astype(jnp.float32)
    for chan in range(CG):
        refs[chan] = ref[chan].astype(jnp.float32)
    for row in range(SPAN):
        start = row // ZL + jnp.where(row % ZL > phase, 1, 0)
        for view in range(2):
            total = jnp.zeros((8, 128), jnp.float32)
            for chan in range(CG):
                line = refs[chan, row : row + 1, :]
                total = total + line * rows[view, chan, pl.ds(start, 8), :]
            out[row, view] = total


def products_call(meta, arrived, ref):
    def spec(view):
        slot = view if arrived.shape[1] == 2 else 0
        return pl.BlockSpec((1, 1, CG, 16, 128), lambda i, m: (m[2 + view], slot, 0, 0, 0))

    return pl.pallas_call(
        products,
        grid_spec=pltpu.PrefetchScalarGridSpec(
            num_scalar_prefetch=1,
            grid=(1,),
            in_specs=[
                spec(0),
                spec(1),
                pl.BlockSpec((CG, SPAN, 128), lambda i, m: (m[6], m[4], 0)),
            ],
            out_specs=pl.BlockSpec((SPAN, 2, 8, 128), lambda i, m: (0, 0, 0, 0)),
            scratch_shapes=[
                pltpu.VMEM((2, CG, 16, 128), jnp.float32),
                pltpu.VMEM((CG, SPAN, 128), jnp.float32),
            ],
        ),
        out_shape=jax.ShapeDtypeStruct((SPAN, 2, 8, 128), jnp.float32),
        name="products",
    )(meta, arrived, arrived, ref)


def weigh(meta, offsets, bands, taps, out):
    sub = lax.broadcasted_iota(jnp.int32, (128, D), 0)
    packed = jnp.zeros((128, D), jnp.float32)
    for view in range(2):
        packed = jnp.where(sub == view, offsets[view : view + 1, :].astype(jnp.float32), packed)
        packed = jnp.where(sub == 2 + view, bands[view : view + 1, :].astype(jnp.float32), packed)
    packed = packed.T
    lane = lax.broadcasted_iota(jnp.int32, (D, 128), 1)
    shift = jnp.bitwise_and(lane // 16 + 4 - jnp.bitwise_and(meta[6], 3), 3)
    reach = (shift + 4 * jnp.bitwise_and(lane, 7)).astype(jnp.float32)
    side = jnp.bitwise_and(lane // 8, 1)
    total = jnp.zeros((D, 128), jnp.float32)
    for view in range(2):
        offset = packed[:, view : view + 1]
        band = packed[:, 2 + view : 3 + view]
        kept = [jnp.where(band > k, taps[view, :, k : k + 1], 0.0) for k in range(4)]
        whole = kept[0] + kept[1] + kept[2] + kept[3]
        lag = jnp.where(side == view, reach, -1.0) - offset
        for k in range(4):
            total = jnp.where(lag == k, kept[k] / whole, total)
    high = total.astype(jnp.bfloat16)
    out[:, :128] = high
    out[:, 128:] = (total - high.astype(jnp.float32)).astype(jnp.bfloat16)


def weigh_call(meta, offsets, bands, taps):
    return pl.pallas_call(
        weigh,
        grid_spec=pltpu.PrefetchScalarGridSpec(
            num_scalar_prefetch=1,
            grid=(1,),
            in_specs=[
                pl.BlockSpec((2, D), lambda i, m: (0, 0)),
                pl.BlockSpec((2, D), lambda i, m: (0, 0)),
                pl.BlockSpec((2, D, 4), lambda i, m: (0, 0, 0)),
            ],
            out_specs=pl.BlockSpec((D, 256), lambda i, m: (0, 0)),
        ),
        out_shape=jax.ShapeDtypeStruct((D, 256), jnp.bfloat16),
        name="weigh",
    )(meta, offsets, bands, taps)


def filtered(filt, weights, pieces, cost, right, left, stack, volume, sums):
    for group in range(G):
        lanes = slice(128 * group, 128 * group + 128)
        for block in range(ZL):
            piece = pieces[block * G + group].reshape(16, 128)
            high = piece.astype(jnp.bfloat16)
            low = (piece - high.astype(jnp.float32)).astype(jnp.bfloat16)
            for copy in range(2):
                at = 128 * copy + 16 * block
                stack[at : at + 16, lanes] = high
                stack[at + 64 : at + 80, lanes] = low
    volume[...] = jnp.dot(weights[...], stack[...], preferred_element_type=jnp.float32)
    zero = jnp.zeros((8, 128), jnp.float32)
    for i in range(3):
        for j in range(3):
            sums[i, j, 0:8, :] = zero
            sums[i, j, D + 8 : D + 16, :] = zero
    step = 32

    def strip(index, carry):
        at = pl.multiple_of(index * step, step)
        totals = [[jnp.zeros((step, 128), jnp.float32) for _ in range(3)] for _ in range(3)]
        for group in range(G):
            part = volume[pl.ds(at, step), 128 * group : 128 * group + 128] * 0.125
            part = part.astype(jnp.bfloat16).astype(jnp.float32)
            for i in range(3):
                for j in range(3):
                    totals[i][j] = totals[i][j] + filt[group * 9 + i * 3 + j] * part
        for i in range(3):
            for j in range(3):
                sums[i, j, pl.ds(at + 8, step), :] = totals[i][j]
        return carry

    lax.fori_loop(0, D // step, strip, 0)
    lane = lax.broadcasted_iota(jnp.int32, (D, 128), 1)
    column = [sums[0, j, 7 : D + 7, :] + sums[1, j, 8 : D + 8, :] + sums[2, j, 9 : D + 9, :] for j in range(3)]
    before = pltpu.roll(column[0], 1, 1)
    after = pltpu.roll(column[2], 127, 1)
    cost[...] = column[1] + jnp.where(lane == 0, 0.0, before) + jnp.where(lane == 127, 0.0, after)
    edges = jnp.where(lane == 0, before, after).T
    right[...] = edges[0:1, :]
    left[...] = edges[127:128, :]


def filtered_call(filt, weights, pieces):
    edge = jax.ShapeDtypeStruct((1, D), jnp.float32)
    return pl.pallas_call(
        filtered,
        in_specs=[
            pl.BlockSpec(memory_space=pltpu.SMEM),
            pl.BlockSpec(memory_space=pltpu.VMEM),
            pl.BlockSpec(memory_space=pltpu.VMEM),
        ],
        out_shape=[jax.ShapeDtypeStruct((D, 128), jnp.float32), edge, edge],
        scratch_shapes=[
            pltpu.VMEM((256, 1024), jnp.bfloat16),
            pltpu.VMEM((D, 1024), jnp.float32),
            pltpu.VMEM((3, 3, D + 16, 128), jnp.float32),
        ],
        name="filtered",
    )(filt, weights, pieces)


def expected(cost, from_left, from_right, out):
    sub = lax.broadcasted_iota(jnp.int32, (128, D), 0)
    edges = jnp.where(sub == 0, from_left[...], jnp.where(sub == 127, from_right[...], 0.0)).T
    whole = cost[...] + edges
    top = jnp.max(whole, axis=0, keepdims=True)
    grown = jnp.exp(whole - top)
    heights = lax.broadcasted_iota(jnp.int32, (D, 128), 0).astype(jnp.float32) * (1.0 / (D - 1))
    out[...] = jnp.sum(grown * heights, axis=0, keepdims=True) / jnp.sum(grown, axis=0, keepdims=True)


def expected_call(cost, from_left, from_right):
    return pl.pallas_call(
        expected,
        out_shape=jax.ShapeDtypeStruct((1, 128), jnp.float32),
        name="expected",
    )(cost, from_left, from_right)


def spread(meta, arrived, ref_feats, picks):
    windows = arrange_call(meta, arrived, picks)
    windows = lax.all_to_all(windows, ("zh", "zl"), 0, 0, tiled=True)
    return products_call(meta, windows, ref_feats)


def body(ref_feats, crops, owner, offsets, bands, taps, filt):
    block = lax.axis_index("zh")
    phase = lax.axis_index("zl")
    group = lax.axis_index("x") * NC + lax.axis_index("c")
    near = owner % G
    far = owner // G
    mine = jnp.where(far[1] == block * ZL + phase, near[1], near[0])
    meta = jnp.stack([near[0], near[1], far[0], far[1], block, phase, group, mine]).astype(jnp.int32)
    arrived = lax.all_to_all(crops[0], ("x", "c"), 0, 0, tiled=True)
    weights = weigh_call(meta, offsets, bands, taps)
    arrived = arrived.reshape(G, CG, 160, 128)
    pieces = lax.cond(
        far[0] == far[1],
        lambda: spread(meta, arrived, ref_feats, (0, 1)),
        lambda: spread(meta, arrived, ref_feats, (7,)),
    )
    pieces = lax.all_to_all(pieces, ("zl", "x", "c"), 0, 0, tiled=True)
    cost, right, left = filtered_call(filt.reshape(G * 9), weights, pieces)
    count = lax.axis_size("ta")
    from_left = lax.ppermute(right, "ta", [(i, i + 1) for i in range(count - 1)])
    from_right = lax.ppermute(left, "ta", [(i + 1, i) for i in range(count - 1)])
    return expected_call(cost, from_left, from_right)


def solution(mesh):
    rows = ("zh", "zl", "x", "c")
    inner = Mesh(mesh.devices.reshape(ZH, ZL, NX, NC, mesh.shape["ta"]), rows + ("ta",))
    placed = (P(None, None, "ta"), P(rows, None, None, "ta"), P(), P(), P(), P(), P())
    return jax.shard_map(body, mesh=inner, in_specs=placed, out_specs=P(rows, "ta"), check_vma=False)
```

```python
import jax
import jax.numpy as jnp
from jax import lax
from jax.experimental import pallas as pl
from jax.experimental.pallas import tpu as pltpu
from jax.sharding import Mesh, PartitionSpec as P

G = 8
CG = 4
D = 256
ZH, ZL, NX, NC = 4, 4, 4, 2
SPAN = 32


def near_core(array):
    return pltpu.with_memory_space_constraint(array, pltpu.VMEM)


def arrange(meta, *refs):
    *sources, out, rows = refs
    for view, source in enumerate(sources):
        for chan in range(CG):
            rows[...] = source[0, chan].astype(jnp.float32)
            for block in range(ZH):
                for phase in range(ZL):
                    picked = rows[pl.ds(SPAN * block + phase, 16, stride=ZL), :]
                    out[block * ZL + phase, view, chan] = picked.astype(jnp.bfloat16)


def arrange_call(meta, arrived, picks):
    def spec(pick):
        return pl.BlockSpec((1, CG, 160, 128), lambda i, m: (m[pick], 0, 0, 0))

    shape = (16, len(picks), CG, 16, 128)
    return pl.pallas_call(
        arrange,
        grid_spec=pltpu.PrefetchScalarGridSpec(
            num_scalar_prefetch=1,
            grid=(1,),
            in_specs=[spec(pick) for pick in picks],
            out_specs=pl.BlockSpec(shape, lambda i, m: (0, 0, 0, 0, 0)),
            scratch_shapes=[pltpu.VMEM((160, 128), jnp.float32)],
        ),
        out_shape=pltpu.VMEM(shape, jnp.bfloat16),
        name="arrange",
    )(meta, *[arrived] * len(picks))


def products(meta, first, second, ref, out, rows, refs):
    phase = meta[5]
    for view, source in enumerate((first, second)):
        for chan in range(CG):
            rows[view, chan] = source[0, 0, chan].astype(jnp.float32)
    for chan in range(CG):
        refs[chan] = ref[chan].astype(jnp.float32)
    for row in range(SPAN):
        start = row // ZL + jnp.where(row % ZL > phase, 1, 0)
        for view in range(2):
            total = jnp.zeros((8, 128), jnp.float32)
            for chan in range(CG):
                line = refs[chan, row : row + 1, :]
                total = total + line * rows[view, chan, pl.ds(start, 8), :]
            out[row, view] = total


def products_call(meta, arrived, ref):
    def spec(view):
        slot = view if arrived.shape[1] == 2 else 0
        return pl.BlockSpec((1, 1, CG, 16, 128), lambda i, m: (m[2 + view], slot, 0, 0, 0))

    return pl.pallas_call(
        products,
        grid_spec=pltpu.PrefetchScalarGridSpec(
            num_scalar_prefetch=1,
            grid=(1,),
            in_specs=[
                spec(0),
                spec(1),
                pl.BlockSpec((CG, SPAN, 128), lambda i, m: (m[6], m[4], 0)),
            ],
            out_specs=pl.BlockSpec((SPAN, 2, 8, 128), lambda i, m: (0, 0, 0, 0)),
            scratch_shapes=[
                pltpu.VMEM((2, CG, 16, 128), jnp.float32),
                pltpu.VMEM((CG, SPAN, 128), jnp.float32),
            ],
        ),
        out_shape=pltpu.VMEM((SPAN, 2, 8, 128), jnp.float32),
        name="products",
    )(meta, arrived, arrived, ref)


def weigh(meta, offsets, bands, taps, out):
    sub = lax.broadcasted_iota(jnp.int32, (128, D), 0)
    packed = jnp.zeros((128, D), jnp.float32)
    for view in range(2):
        packed = jnp.where(sub == view, offsets[view : view + 1, :].astype(jnp.float32), packed)
        packed = jnp.where(sub == 2 + view, bands[view : view + 1, :].astype(jnp.float32), packed)
    packed = packed.T
    lane = lax.broadcasted_iota(jnp.int32, (D, 128), 1)
    shift = jnp.bitwise_and(lane // 16 + 4 - jnp.bitwise_and(meta[6], 3), 3)
    reach = (shift + 4 * jnp.bitwise_and(lane, 7)).astype(jnp.float32)
    side = jnp.bitwise_and(lane // 8, 1)
    total = jnp.zeros((D, 128), jnp.float32)
    for view in range(2):
        offset = packed[:, view : view + 1]
        band = packed[:, 2 + view : 3 + view]
        kept = [jnp.where(band > k, taps[view, :, k : k + 1], 0.0) for k in range(4)]
        whole = kept[0] + kept[1] + kept[2] + kept[3]
        lag = jnp.where(side == view, reach, -1.0) - offset
        for k in range(4):
            total = jnp.where(lag == k, kept[k] / whole, total)
    high = total.astype(jnp.bfloat16)
    out[:, :128] = high
    out[:, 128:] = (total - high.astype(jnp.float32)).astype(jnp.bfloat16)


def weigh_call(meta, offsets, bands, taps):
    return pl.pallas_call(
        weigh,
        grid_spec=pltpu.PrefetchScalarGridSpec(
            num_scalar_prefetch=1,
            grid=(1,),
            in_specs=[
                pl.BlockSpec((2, D), lambda i, m: (0, 0)),
                pl.BlockSpec((2, D), lambda i, m: (0, 0)),
                pl.BlockSpec((2, D, 4), lambda i, m: (0, 0, 0)),
            ],
            out_specs=pl.BlockSpec((D, 256), lambda i, m: (0, 0)),
        ),
        out_shape=pltpu.VMEM((D, 256), jnp.bfloat16),
        name="weigh",
    )(meta, offsets, bands, taps)


def filtered(filt, weights, pieces, cost, right, left, stack, volume, sums):
    for group in range(G):
        lanes = slice(128 * group, 128 * group + 128)
        for block in range(ZL):
            piece = pieces[block * G + group].reshape(16, 128)
            high = piece.astype(jnp.bfloat16)
            low = (piece - high.astype(jnp.float32)).astype(jnp.bfloat16)
            for copy in range(2):
                at = 128 * copy + 16 * block
                stack[at : at + 16, lanes] = high
                stack[at + 64 : at + 80, lanes] = low
    volume[...] = jnp.dot(weights[...], stack[...], preferred_element_type=jnp.float32)
    zero = jnp.zeros((8, 128), jnp.float32)
    for i in range(3):
        for j in range(3):
            sums[i, j, 0:8, :] = zero
            sums[i, j, D + 8 : D + 16, :] = zero
    step = 32

    def strip(index, carry):
        at = pl.multiple_of(index * step, step)
        totals = [[jnp.zeros((step, 128), jnp.float32) for _ in range(3)] for _ in range(3)]
        for group in range(G):
            part = volume[pl.ds(at, step), 128 * group : 128 * group + 128] * 0.125
            part = part.astype(jnp.bfloat16).astype(jnp.float32)
            for i in range(3):
                for j in range(3):
                    totals[i][j] = totals[i][j] + filt[group * 9 + i * 3 + j] * part
        for i in range(3):
            for j in range(3):
                sums[i, j, pl.ds(at + 8, step), :] = totals[i][j]
        return carry

    lax.fori_loop(0, D // step, strip, 0)
    lane = lax.broadcasted_iota(jnp.int32, (D, 128), 1)
    column = [sums[0, j, 7 : D + 7, :] + sums[1, j, 8 : D + 8, :] + sums[2, j, 9 : D + 9, :] for j in range(3)]
    before = pltpu.roll(column[0], 1, 1)
    after = pltpu.roll(column[2], 127, 1)
    cost[...] = column[1] + jnp.where(lane == 0, 0.0, before) + jnp.where(lane == 127, 0.0, after)
    edges = jnp.where(lane == 0, before, after).T
    right[...] = edges[0:1, :]
    left[...] = edges[127:128, :]


def filtered_call(filt, weights, pieces):
    edge = pltpu.VMEM((1, D), jnp.float32)
    return pl.pallas_call(
        filtered,
        in_specs=[
            pl.BlockSpec(memory_space=pltpu.SMEM),
            pl.BlockSpec(memory_space=pltpu.VMEM),
            pl.BlockSpec(memory_space=pltpu.VMEM),
        ],
        out_shape=[pltpu.VMEM((D, 128), jnp.float32), edge, edge],
        scratch_shapes=[
            pltpu.VMEM((256, 1024), jnp.bfloat16),
            pltpu.VMEM((D, 1024), jnp.float32),
            pltpu.VMEM((3, 3, D + 16, 128), jnp.float32),
        ],
        name="filtered",
    )(filt, weights, pieces)


def expected(cost, from_left, from_right, out):
    sub = lax.broadcasted_iota(jnp.int32, (128, D), 0)
    edges = jnp.where(sub == 0, from_left[...], jnp.where(sub == 127, from_right[...], 0.0)).T
    whole = cost[...] + edges
    top = jnp.max(whole, axis=0, keepdims=True)
    grown = jnp.exp(whole - top)
    heights = lax.broadcasted_iota(jnp.int32, (D, 128), 0).astype(jnp.float32) * (1.0 / (D - 1))
    out[...] = jnp.sum(grown * heights, axis=0, keepdims=True) / jnp.sum(grown, axis=0, keepdims=True)


def expected_call(cost, from_left, from_right):
    return pl.pallas_call(
        expected,
        out_shape=jax.ShapeDtypeStruct((1, 128), jnp.float32),
        name="expected",
    )(cost, from_left, from_right)


def spread(meta, arrived, ref_feats, picks):
    windows = arrange_call(meta, arrived, picks)
    windows = lax.all_to_all(windows, ("zh", "zl"), 0, 0, tiled=True)
    return products_call(meta, near_core(windows), ref_feats)


def body(ref_feats, crops, owner, offsets, bands, taps, filt):
    block = lax.axis_index("zh")
    phase = lax.axis_index("zl")
    group = lax.axis_index("x") * NC + lax.axis_index("c")
    near = owner % G
    far = owner // G
    mine = jnp.where(far[1] == block * ZL + phase, near[1], near[0])
    meta = jnp.stack([near[0], near[1], far[0], far[1], block, phase, group, mine]).astype(jnp.int32)
    arrived = lax.all_to_all(crops[0], ("x", "c"), 0, 0, tiled=True)
    weights = weigh_call(meta, offsets, bands, taps)
    arrived = near_core(arrived.reshape(G, CG, 160, 128))
    pieces = lax.cond(
        far[0] == far[1],
        lambda: spread(meta, arrived, ref_feats, (0, 1)),
        lambda: spread(meta, arrived, ref_feats, (7,)),
    )
    pieces = lax.all_to_all(pieces, ("zl", "x", "c"), 0, 0, tiled=True)
    cost, right, left = filtered_call(filt.reshape(G * 9), near_core(weights), near_core(pieces))
    count = lax.axis_size("ta")
    from_left = lax.ppermute(right, "ta", [(i, i + 1) for i in range(count - 1)])
    from_right = lax.ppermute(left, "ta", [(i + 1, i) for i in range(count - 1)])
    return expected_call(near_core(cost), near_core(from_left), near_core(from_right))


def solution(mesh):
    rows = ("zh", "zl", "x", "c")
    inner = Mesh(mesh.devices.reshape(ZH, ZL, NX, NC, mesh.shape["ta"]), rows + ("ta",))
    placed = (P(None, None, "ta"), P(rows, None, None, "ta"), P(), P(), P(), P(), P())
    return jax.shard_map(body, mesh=inner, in_specs=placed, out_specs=P(rows, "ta"), check_vma=False)
```

```python
import jax
import jax.numpy as jnp
from jax import lax
from jax.experimental import pallas as pl
from jax.experimental.pallas import tpu as pltpu
from jax.sharding import Mesh, PartitionSpec as P

G = 8
CG = 4
D = 256
ZH, ZL, NX, NC = 4, 4, 4, 2
SPAN = 32


def near_core(array):
    return pltpu.with_memory_space_constraint(array, pltpu.VMEM)


def arrange(meta, *refs):
    *sources, out, rows = refs
    for view, source in enumerate(sources):
        for chan in range(CG):
            rows[...] = source[0, chan].astype(jnp.float32)
            for block in range(ZH):
                for phase in range(ZL):
                    picked = rows[pl.ds(SPAN * block + phase, 16, stride=ZL), :]
                    out[block * ZL + phase, view, chan] = picked.astype(jnp.bfloat16)


def arrange_call(meta, arrived, picks):
    def spec(pick):
        return pl.BlockSpec((1, CG, 160, 128), lambda i, m: (m[pick], 0, 0, 0))

    shape = (16, len(picks), CG, 16, 128)
    return pl.pallas_call(
        arrange,
        grid_spec=pltpu.PrefetchScalarGridSpec(
            num_scalar_prefetch=1,
            grid=(1,),
            in_specs=[spec(pick) for pick in picks],
            out_specs=pl.BlockSpec(shape, lambda i, m: (0, 0, 0, 0, 0)),
            scratch_shapes=[pltpu.VMEM((160, 128), jnp.float32)],
        ),
        out_shape=pltpu.VMEM(shape, jnp.bfloat16),
        name="arrange",
    )(meta, *[arrived] * len(picks))


def products(meta, first, second, ref, out, rows, refs):
    phase = meta[5]
    for view, source in enumerate((first, second)):
        for chan in range(CG):
            rows[view, chan] = source[0, 0, chan].astype(jnp.float32)
    for chan in range(CG):
        refs[chan] = ref[chan].astype(jnp.float32)
    for row in range(SPAN):
        start = row // ZL + jnp.where(row % ZL > phase, 1, 0)
        for view in range(2):
            total = jnp.zeros((8, 128), jnp.float32)
            for chan in range(CG):
                line = refs[chan, row : row + 1, :]
                total = total + line * rows[view, chan, pl.ds(start, 8), :]
            out[row, view] = total


def products_call(meta, arrived, ref):
    def spec(view):
        slot = view if arrived.shape[1] == 2 else 0
        return pl.BlockSpec((1, 1, CG, 16, 128), lambda i, m: (m[2 + view], slot, 0, 0, 0))

    return pl.pallas_call(
        products,
        grid_spec=pltpu.PrefetchScalarGridSpec(
            num_scalar_prefetch=1,
            grid=(1,),
            in_specs=[
                spec(0),
                spec(1),
                pl.BlockSpec((CG, SPAN, 128), lambda i, m: (m[6], m[4], 0)),
            ],
            out_specs=pl.BlockSpec((SPAN, 2, 8, 128), lambda i, m: (0, 0, 0, 0)),
            scratch_shapes=[
                pltpu.VMEM((2, CG, 16, 128), jnp.float32),
                pltpu.VMEM((CG, SPAN, 128), jnp.float32),
            ],
        ),
        out_shape=pltpu.VMEM((SPAN, 2, 8, 128), jnp.float32),
        name="products",
    )(meta, arrived, arrived, ref)


def weigh(meta, offsets, bands, taps, out):
    sub = lax.broadcasted_iota(jnp.int32, (128, D), 0)
    packed = jnp.zeros((128, D), jnp.float32)
    for view in range(2):
        packed = jnp.where(sub == view, offsets[view : view + 1, :].astype(jnp.float32), packed)
        packed = jnp.where(sub == 2 + view, bands[view : view + 1, :].astype(jnp.float32), packed)
    packed = packed.T
    lane = lax.broadcasted_iota(jnp.int32, (D, 128), 1)
    shift = jnp.bitwise_and(lane // 16 + 4 - jnp.bitwise_and(meta[6], 3), 3)
    reach = (shift + 4 * jnp.bitwise_and(lane, 7)).astype(jnp.float32)
    side = jnp.bitwise_and(lane // 8, 1)
    total = jnp.zeros((D, 128), jnp.float32)
    for view in range(2):
        offset = packed[:, view : view + 1]
        band = packed[:, 2 + view : 3 + view]
        kept = [jnp.where(band > k, taps[view, :, k : k + 1], 0.0) for k in range(4)]
        whole = kept[0] + kept[1] + kept[2] + kept[3]
        lag = jnp.where(side == view, reach, -1.0) - offset
        for k in range(4):
            total = jnp.where(lag == k, kept[k] / whole, total)
    high = total.astype(jnp.bfloat16)
    out[:, :128] = high
    out[:, 128:] = (total - high.astype(jnp.float32)).astype(jnp.bfloat16)


def weigh_call(meta, offsets, bands, taps):
    return pl.pallas_call(
        weigh,
        grid_spec=pltpu.PrefetchScalarGridSpec(
            num_scalar_prefetch=1,
            grid=(1,),
            in_specs=[
                pl.BlockSpec((2, D), lambda i, m: (0, 0)),
                pl.BlockSpec((2, D), lambda i, m: (0, 0)),
                pl.BlockSpec((2, D, 4), lambda i, m: (0, 0, 0)),
            ],
            out_specs=pl.BlockSpec((D, 256), lambda i, m: (0, 0)),
        ),
        out_shape=pltpu.VMEM((D, 256), jnp.bfloat16),
        name="weigh",
    )(meta, offsets, bands, taps)


def brink(filt, weights, pieces, right, left, stack, sums):
    lane = lax.broadcasted_iota(jnp.int32, (16, 128), 1)
    for block in range(ZL):
        ends = jnp.zeros((16, 128), jnp.float32)
        for group in range(G):
            piece = pieces[block * G + group].reshape(16, 128)
            ends = jnp.where(lane == group, pltpu.roll(piece, group + 1, 1), ends)
            ends = jnp.where(lane == G + group, pltpu.roll(piece, G + group, 1), ends)
        high = ends.astype(jnp.bfloat16)
        low = (ends - high.astype(jnp.float32)).astype(jnp.bfloat16)
        for copy in range(2):
            at = 128 * copy + 16 * block
            stack[at : at + 16, :] = high
            stack[at + 64 : at + 80, :] = low
    part = jnp.dot(weights[...], stack[...], preferred_element_type=jnp.float32) * 0.125
    part = part.astype(jnp.bfloat16).astype(jnp.float32)
    slot = lax.broadcasted_iota(jnp.int32, (1, 128), 1)
    zero = jnp.zeros((8, 128), jnp.float32)
    for i in range(3):
        line = jnp.zeros((1, 128), jnp.float32)
        for group in range(G):
            line = jnp.where(slot == group, filt[group * 9 + i * 3], line)
            line = jnp.where(slot == G + group, filt[group * 9 + i * 3 + 2], line)
        sums[i, 0:8, :] = zero
        sums[i, D + 8 : D + 16, :] = zero
        sums[i, 8 : D + 8, :] = part * line
    total = (sums[0, 7 : D + 7, :] + sums[1, 8 : D + 8, :] + sums[2, 9 : D + 9, :]).T
    right[...] = jnp.sum(total[0:G], axis=0, keepdims=True)
    left[...] = jnp.sum(total[G : 2 * G], axis=0, keepdims=True)


def brink_call(filt, weights, pieces):
    edge = pltpu.VMEM((1, D), jnp.float32)
    return pl.pallas_call(
        brink,
        in_specs=[
            pl.BlockSpec(memory_space=pltpu.SMEM),
            pl.BlockSpec(memory_space=pltpu.VMEM),
            pl.BlockSpec(memory_space=pltpu.VMEM),
        ],
        out_shape=[edge, edge],
        scratch_shapes=[pltpu.VMEM((256, 128), jnp.bfloat16), pltpu.VMEM((3, D + 16, 128), jnp.float32)],
        name="brink",
    )(filt, weights, pieces)


def filtered(filt, weights, pieces, cost, stack, volume, sums):
    for group in range(G):
        lanes = slice(128 * group, 128 * group + 128)
        for block in range(ZL):
            piece = pieces[block * G + group].reshape(16, 128)
            high = piece.astype(jnp.bfloat16)
            low = (piece - high.astype(jnp.float32)).astype(jnp.bfloat16)
            for copy in range(2):
                at = 128 * copy + 16 * block
                stack[at : at + 16, lanes] = high
                stack[at + 64 : at + 80, lanes] = low
    volume[...] = jnp.dot(weights[...], stack[...], preferred_element_type=jnp.float32)
    zero = jnp.zeros((8, 128), jnp.float32)
    for i in range(3):
        for j in range(3):
            sums[i, j, 0:8, :] = zero
            sums[i, j, D + 8 : D + 16, :] = zero
    step = 32

    def strip(index, carry):
        at = pl.multiple_of(index * step, step)
        totals = [[jnp.zeros((step, 128), jnp.float32) for _ in range(3)] for _ in range(3)]
        for group in range(G):
            part = volume[pl.ds(at, step), 128 * group : 128 * group + 128] * 0.125
            part = part.astype(jnp.bfloat16).astype(jnp.float32)
            for i in range(3):
                for j in range(3):
                    totals[i][j] = totals[i][j] + filt[group * 9 + i * 3 + j] * part
        for i in range(3):
            for j in range(3):
                sums[i, j, pl.ds(at + 8, step), :] = totals[i][j]
        return carry

    lax.fori_loop(0, D // step, strip, 0)
    lane = lax.broadcasted_iota(jnp.int32, (D, 128), 1)
    column = [sums[0, j, 7 : D + 7, :] + sums[1, j, 8 : D + 8, :] + sums[2, j, 9 : D + 9, :] for j in range(3)]
    before = pltpu.roll(column[0], 1, 1)
    after = pltpu.roll(column[2], 127, 1)
    cost[...] = column[1] + jnp.where(lane == 0, 0.0, before) + jnp.where(lane == 127, 0.0, after)


def filtered_call(filt, weights, pieces):
    return pl.pallas_call(
        filtered,
        in_specs=[
            pl.BlockSpec(memory_space=pltpu.SMEM),
            pl.BlockSpec(memory_space=pltpu.VMEM),
            pl.BlockSpec(memory_space=pltpu.VMEM),
        ],
        out_shape=pltpu.VMEM((D, 128), jnp.float32),
        scratch_shapes=[
            pltpu.VMEM((256, 1024), jnp.bfloat16),
            pltpu.VMEM((D, 1024), jnp.float32),
            pltpu.VMEM((3, 3, D + 16, 128), jnp.float32),
        ],
        name="filtered",
    )(filt, weights, pieces)


def expected(cost, from_left, from_right, out):
    sub = lax.broadcasted_iota(jnp.int32, (128, D), 0)
    edges = jnp.where(sub == 0, from_left[...], jnp.where(sub == 127, from_right[...], 0.0)).T
    whole = cost[...] + edges
    top = jnp.max(whole, axis=0, keepdims=True)
    grown = jnp.exp(whole - top)
    heights = lax.broadcasted_iota(jnp.int32, (D, 128), 0).astype(jnp.float32) * (1.0 / (D - 1))
    out[...] = jnp.sum(grown * heights, axis=0, keepdims=True) / jnp.sum(grown, axis=0, keepdims=True)


def expected_call(cost, from_left, from_right):
    return pl.pallas_call(
        expected,
        out_shape=jax.ShapeDtypeStruct((1, 128), jnp.float32),
        name="expected",
    )(cost, from_left, from_right)


def spread(meta, arrived, ref_feats, picks):
    windows = arrange_call(meta, arrived, picks)
    windows = lax.all_to_all(windows, ("zh", "zl"), 0, 0, tiled=True)
    return products_call(meta, near_core(windows), ref_feats)


def body(ref_feats, crops, owner, offsets, bands, taps, filt):
    block = lax.axis_index("zh")
    phase = lax.axis_index("zl")
    group = lax.axis_index("x") * NC + lax.axis_index("c")
    near = owner % G
    far = owner // G
    mine = jnp.where(far[1] == block * ZL + phase, near[1], near[0])
    meta = jnp.stack([near[0], near[1], far[0], far[1], block, phase, group, mine]).astype(jnp.int32)
    arrived = lax.all_to_all(crops[0], ("x", "c"), 0, 0, tiled=True)
    weights = weigh_call(meta, offsets, bands, taps)
    arrived = near_core(arrived.reshape(G, CG, 160, 128))
    pieces = lax.cond(
        far[0] == far[1],
        lambda: spread(meta, arrived, ref_feats, (0, 1)),
        lambda: spread(meta, arrived, ref_feats, (7,)),
    )
    pieces = lax.all_to_all(pieces, ("zl", "x", "c"), 0, 0, tiled=True)
    filt = filt.reshape(G * 9)
    weights = near_core(weights)
    pieces = near_core(pieces)
    right, left = brink_call(filt, weights, pieces)
    count = lax.axis_size("ta")
    from_left = lax.ppermute(right, "ta", [(i, i + 1) for i in range(count - 1)])
    from_right = lax.ppermute(left, "ta", [(i + 1, i) for i in range(count - 1)])
    cost = filtered_call(filt, weights, pieces)
    return expected_call(near_core(cost), near_core(from_left), near_core(from_right))


def solution(mesh):
    rows = ("zh", "zl", "x", "c")
    inner = Mesh(mesh.devices.reshape(ZH, ZL, NX, NC, mesh.shape["ta"]), rows + ("ta",))
    placed = (P(None, None, "ta"), P(rows, None, None, "ta"), P(), P(), P(), P(), P())
    return jax.shard_map(body, mesh=inner, in_specs=placed, out_specs=P(rows, "ta"), check_vma=False)
```

```python
import jax
import jax.numpy as jnp
from jax import lax
from jax.experimental import pallas as pl
from jax.experimental.pallas import tpu as pltpu
from jax.sharding import Mesh, PartitionSpec as P

G = 8
CG = 4
D = 256
ZH, ZL, NX, NC = 4, 4, 4, 2
SPAN = 32


def near_core(array):
    return pltpu.with_memory_space_constraint(array, pltpu.VMEM)


def arrange(meta, *refs):
    *sources, out, rows = refs
    for view, source in enumerate(sources):
        for chan in range(CG):
            rows[...] = source[0, chan].astype(jnp.float32)
            for block in range(ZH):
                for phase in range(ZL):
                    picked = rows[pl.ds(SPAN * block + phase, 16, stride=ZL), :]
                    out[block * ZL + phase, view, chan] = picked.astype(jnp.bfloat16)


def arrange_call(meta, arrived, picks):
    def spec(pick):
        return pl.BlockSpec((1, CG, 160, 128), lambda i, m: (m[pick], 0, 0, 0))

    shape = (16, len(picks), CG, 16, 128)
    return pl.pallas_call(
        arrange,
        grid_spec=pltpu.PrefetchScalarGridSpec(
            num_scalar_prefetch=1,
            grid=(1,),
            in_specs=[spec(pick) for pick in picks],
            out_specs=pl.BlockSpec(shape, lambda i, m: (0, 0, 0, 0, 0)),
            scratch_shapes=[pltpu.VMEM((160, 128), jnp.float32)],
        ),
        out_shape=pltpu.VMEM(shape, jnp.bfloat16),
        name="arrange",
    )(meta, *[arrived] * len(picks))


def products(meta, first, second, ref, out, rows, refs):
    phase = meta[5]
    for view, source in enumerate((first, second)):
        for chan in range(CG):
            rows[view, chan] = source[0, 0, chan].astype(jnp.float32)
    for chan in range(CG):
        refs[chan] = ref[chan].astype(jnp.float32)
    for row in range(SPAN):
        start = row // ZL + jnp.where(row % ZL > phase, 1, 0)
        totals = []
        for view in range(2):
            total = jnp.zeros((8, 128), jnp.float32)
            for chan in range(CG):
                line = refs[chan, row : row + 1, :]
                total = total + line * rows[view, chan, pl.ds(start, 8), :]
            totals.append(total)
        out[row] = jnp.concatenate(totals, axis=0)


def products_call(meta, arrived, ref):
    def spec(view):
        slot = view if arrived.shape[1] == 2 else 0
        return pl.BlockSpec((1, 1, CG, 16, 128), lambda i, m: (m[2 + view], slot, 0, 0, 0))

    return pl.pallas_call(
        products,
        grid_spec=pltpu.PrefetchScalarGridSpec(
            num_scalar_prefetch=1,
            grid=(1,),
            in_specs=[
                spec(0),
                spec(1),
                pl.BlockSpec((CG, SPAN, 128), lambda i, m: (m[6], m[4], 0)),
            ],
            out_specs=pl.BlockSpec((SPAN, 16, 128), lambda i, m: (0, 0, 0)),
            scratch_shapes=[
                pltpu.VMEM((2, CG, 16, 128), jnp.float32),
                pltpu.VMEM((CG, SPAN, 128), jnp.float32),
            ],
        ),
        out_shape=pltpu.VMEM((SPAN, 16, 128), jnp.float32),
        name="products",
    )(meta, arrived, arrived, ref)


def weigh(meta, offsets, bands, taps, out):
    sub = lax.broadcasted_iota(jnp.int32, (128, D), 0)
    packed = jnp.zeros((128, D), jnp.float32)
    for view in range(2):
        packed = jnp.where(sub == view, offsets[view : view + 1, :].astype(jnp.float32), packed)
        packed = jnp.where(sub == 2 + view, bands[view : view + 1, :].astype(jnp.float32), packed)
    packed = packed.T
    lane = lax.broadcasted_iota(jnp.int32, (D, 128), 1)
    shift = jnp.bitwise_and(lane // 16 + 4 - jnp.bitwise_and(meta[6], 3), 3)
    reach = (shift + 4 * jnp.bitwise_and(lane, 7)).astype(jnp.float32)
    side = jnp.bitwise_and(lane // 8, 1)
    total = jnp.zeros((D, 128), jnp.float32)
    for view in range(2):
        offset = packed[:, view : view + 1]
        band = packed[:, 2 + view : 3 + view]
        kept = [jnp.where(band > k, taps[view, :, k : k + 1], 0.0) for k in range(4)]
        whole = kept[0] + kept[1] + kept[2] + kept[3]
        lag = jnp.where(side == view, reach, -1.0) - offset
        for k in range(4):
            total = jnp.where(lag == k, kept[k] / whole, total)
    high = total.astype(jnp.bfloat16)
    out[:, :128] = high
    out[:, 128:] = (total - high.astype(jnp.float32)).astype(jnp.bfloat16)


def weigh_call(meta, offsets, bands, taps):
    return pl.pallas_call(
        weigh,
        grid_spec=pltpu.PrefetchScalarGridSpec(
            num_scalar_prefetch=1,
            grid=(1,),
            in_specs=[
                pl.BlockSpec((2, D), lambda i, m: (0, 0)),
                pl.BlockSpec((2, D), lambda i, m: (0, 0)),
                pl.BlockSpec((2, D, 4), lambda i, m: (0, 0, 0)),
            ],
            out_specs=pl.BlockSpec((D, 256), lambda i, m: (0, 0)),
        ),
        out_shape=pltpu.VMEM((D, 256), jnp.bfloat16),
        name="weigh",
    )(meta, offsets, bands, taps)


def brink(filt, weights, pieces, right, left, stack, sums):
    lane = lax.broadcasted_iota(jnp.int32, (16, 128), 1)
    for block in range(ZL):
        ends = jnp.zeros((16, 128), jnp.float32)
        for group in range(G):
            piece = pieces[block * G + group]
            ends = jnp.where(lane == group, pltpu.roll(piece, group + 1, 1), ends)
            ends = jnp.where(lane == G + group, pltpu.roll(piece, G + group, 1), ends)
        high = ends.astype(jnp.bfloat16)
        low = (ends - high.astype(jnp.float32)).astype(jnp.bfloat16)
        for copy in range(2):
            at = 128 * copy + 16 * block
            stack[at : at + 16, :] = high
            stack[at + 64 : at + 80, :] = low
    part = jnp.dot(weights[...], stack[...], preferred_element_type=jnp.float32) * 0.125
    part = part.astype(jnp.bfloat16).astype(jnp.float32)
    slot = lax.broadcasted_iota(jnp.int32, (1, 128), 1)
    zero = jnp.zeros((8, 128), jnp.float32)
    for i in range(3):
        line = jnp.zeros((1, 128), jnp.float32)
        for group in range(G):
            line = jnp.where(slot == group, filt[group * 9 + i * 3], line)
            line = jnp.where(slot == G + group, filt[group * 9 + i * 3 + 2], line)
        sums[i, 0:8, :] = zero
        sums[i, D + 8 : D + 16, :] = zero
        sums[i, 8 : D + 8, :] = part * line
    total = (sums[0, 7 : D + 7, :] + sums[1, 8 : D + 8, :] + sums[2, 9 : D + 9, :]).T
    right[...] = jnp.sum(total[0:G], axis=0, keepdims=True)
    left[...] = jnp.sum(total[G : 2 * G], axis=0, keepdims=True)


def brink_call(filt, weights, pieces):
    edge = pltpu.VMEM((1, D), jnp.float32)
    return pl.pallas_call(
        brink,
        in_specs=[
            pl.BlockSpec(memory_space=pltpu.SMEM),
            pl.BlockSpec(memory_space=pltpu.VMEM),
            pl.BlockSpec(memory_space=pltpu.VMEM),
        ],
        out_shape=[edge, edge],
        scratch_shapes=[pltpu.VMEM((256, 128), jnp.bfloat16), pltpu.VMEM((3, D + 16, 128), jnp.float32)],
        name="brink",
    )(filt, weights, pieces)


def filtered(filt, weights, pieces, cost, stack, volume, sums):
    for group in range(G):
        lanes = slice(128 * group, 128 * group + 128)
        for block in range(ZL):
            piece = pieces[block * G + group]
            high = piece.astype(jnp.bfloat16)
            low = (piece - high.astype(jnp.float32)).astype(jnp.bfloat16)
            for copy in range(2):
                at = 128 * copy + 16 * block
                stack[at : at + 16, lanes] = high
                stack[at + 64 : at + 80, lanes] = low
    volume[...] = jnp.dot(weights[...], stack[...], preferred_element_type=jnp.float32)
    zero = jnp.zeros((8, 128), jnp.float32)
    for i in range(3):
        for j in range(3):
            sums[i, j, 0:8, :] = zero
            sums[i, j, D + 8 : D + 16, :] = zero
    step = 32

    def strip(index, carry):
        at = pl.multiple_of(index * step, step)
        totals = [[jnp.zeros((step, 128), jnp.float32) for _ in range(3)] for _ in range(3)]
        for group in range(G):
            part = volume[pl.ds(at, step), 128 * group : 128 * group + 128] * 0.125
            part = part.astype(jnp.bfloat16).astype(jnp.float32)
            for i in range(3):
                for j in range(3):
                    totals[i][j] = totals[i][j] + filt[group * 9 + i * 3 + j] * part
        for i in range(3):
            for j in range(3):
                sums[i, j, pl.ds(at + 8, step), :] = totals[i][j]
        return carry

    lax.fori_loop(0, D // step, strip, 0)
    lane = lax.broadcasted_iota(jnp.int32, (D, 128), 1)
    column = [sums[0, j, 7 : D + 7, :] + sums[1, j, 8 : D + 8, :] + sums[2, j, 9 : D + 9, :] for j in range(3)]
    before = pltpu.roll(column[0], 1, 1)
    after = pltpu.roll(column[2], 127, 1)
    cost[...] = column[1] + jnp.where(lane == 0, 0.0, before) + jnp.where(lane == 127, 0.0, after)


def filtered_call(filt, weights, pieces):
    return pl.pallas_call(
        filtered,
        in_specs=[
            pl.BlockSpec(memory_space=pltpu.SMEM),
            pl.BlockSpec(memory_space=pltpu.VMEM),
            pl.BlockSpec(memory_space=pltpu.VMEM),
        ],
        out_shape=pltpu.VMEM((D, 128), jnp.float32),
        scratch_shapes=[
            pltpu.VMEM((256, 1024), jnp.bfloat16),
            pltpu.VMEM((D, 1024), jnp.float32),
            pltpu.VMEM((3, 3, D + 16, 128), jnp.float32),
        ],
        name="filtered",
    )(filt, weights, pieces)


def expected(cost, from_left, from_right, out):
    sub = lax.broadcasted_iota(jnp.int32, (128, D), 0)
    edges = jnp.where(sub == 0, from_left[...], jnp.where(sub == 127, from_right[...], 0.0)).T
    whole = cost[...] + edges
    top = jnp.max(whole, axis=0, keepdims=True)
    grown = jnp.exp(whole - top)
    heights = lax.broadcasted_iota(jnp.int32, (D, 128), 0).astype(jnp.float32) * (1.0 / (D - 1))
    out[...] = jnp.sum(grown * heights, axis=0, keepdims=True) / jnp.sum(grown, axis=0, keepdims=True)


def expected_call(cost, from_left, from_right):
    return pl.pallas_call(
        expected,
        out_shape=jax.ShapeDtypeStruct((1, 128), jnp.float32),
        name="expected",
    )(cost, from_left, from_right)


def spread(meta, arrived, ref_feats, picks):
    windows = arrange_call(meta, arrived, picks)
    windows = lax.all_to_all(windows, ("zh", "zl"), 0, 0, tiled=True)
    return products_call(meta, near_core(windows), ref_feats)


def body(ref_feats, crops, owner, offsets, bands, taps, filt):
    block = lax.axis_index("zh")
    phase = lax.axis_index("zl")
    group = lax.axis_index("x") * NC + lax.axis_index("c")
    near = owner % G
    far = owner // G
    mine = jnp.where(far[1] == block * ZL + phase, near[1], near[0])
    meta = jnp.stack([near[0], near[1], far[0], far[1], block, phase, group, mine]).astype(jnp.int32)
    arrived = lax.all_to_all(crops[0], ("x", "c"), 0, 0, tiled=True)
    weights = weigh_call(meta, offsets, bands, taps)
    arrived = near_core(arrived.reshape(G, CG, 160, 128))
    pieces = lax.cond(
        jnp.logical_and(far[0] == far[1], near[0] != near[1]),
        lambda: spread(meta, arrived, ref_feats, (0, 1)),
        lambda: spread(meta, arrived, ref_feats, (7,)),
    )
    pieces = lax.all_to_all(pieces.astype(jnp.float16), ("zl", "x", "c"), 0, 0, tiled=True)
    pieces = pieces.astype(jnp.float32)
    filt = filt.reshape(G * 9)
    weights = near_core(weights)
    pieces = near_core(pieces)
    right, left = brink_call(filt, weights, pieces)
    count = lax.axis_size("ta")
    from_left = lax.ppermute(right, "ta", [(i, i + 1) for i in range(count - 1)])
    from_right = lax.ppermute(left, "ta", [(i + 1, i) for i in range(count - 1)])
    cost = filtered_call(filt, weights, pieces)
    return expected_call(near_core(cost), near_core(from_left), near_core(from_right))


def solution(mesh):
    rows = ("zh", "zl", "x", "c")
    inner = Mesh(mesh.devices.reshape(ZH, ZL, NX, NC, mesh.shape["ta"]), rows + ("ta",))
    placed = (P(None, None, "ta"), P(rows, None, None, "ta"), P(), P(), P(), P(), P())
    return jax.shard_map(body, mesh=inner, in_specs=placed, out_specs=P(rows, "ta"), check_vma=False)
```

```python
import jax
import jax.numpy as jnp
from jax import lax
from jax.experimental import pallas as pl
from jax.experimental.pallas import tpu as pltpu
from jax.sharding import Mesh, PartitionSpec as P

G = 8
CG = 4
D = 256
ZH, ZL, NX, NC = 4, 4, 4, 2
SPAN = 32


def near_core(array):
    return pltpu.with_memory_space_constraint(array, pltpu.VMEM)


def arrange(meta, *refs):
    *sources, out, rows = refs
    for view, source in enumerate(sources):
        for chan in range(CG):
            rows[...] = source[0, chan].astype(jnp.float32)
            for block in range(ZH):
                for phase in range(ZL):
                    picked = rows[pl.ds(SPAN * block + phase, 16, stride=ZL), :]
                    out[block * ZL + phase, view, chan] = picked.astype(jnp.bfloat16)


def arrange_call(meta, arrived, picks):
    def spec(pick):
        return pl.BlockSpec((1, CG, 160, 128), lambda i, m: (m[pick], 0, 0, 0))

    shape = (16, len(picks), CG, 16, 128)
    return pl.pallas_call(
        arrange,
        grid_spec=pltpu.PrefetchScalarGridSpec(
            num_scalar_prefetch=1,
            grid=(1,),
            in_specs=[spec(pick) for pick in picks],
            out_specs=pl.BlockSpec(shape, lambda i, m: (0, 0, 0, 0, 0)),
            scratch_shapes=[pltpu.VMEM((160, 128), jnp.float32)],
        ),
        out_shape=pltpu.VMEM(shape, jnp.bfloat16),
        name="arrange",
    )(meta, *[arrived] * len(picks))


def products(meta, first, second, ref, out, rows, refs):
    phase = meta[5]
    for view, source in enumerate((first, second)):
        for chan in range(CG):
            rows[view, chan] = source[0, 0, chan].astype(jnp.float32)
    for chan in range(CG):
        refs[chan] = ref[chan].astype(jnp.float32)
    for row in range(SPAN):
        start = row // ZL + jnp.where(row % ZL > phase, 1, 0)
        totals = []
        for view in range(2):
            total = jnp.zeros((8, 128), jnp.float32)
            for chan in range(CG):
                line = refs[chan, row : row + 1, :]
                total = total + line * rows[view, chan, pl.ds(start, 8), :]
            totals.append(total)
        out[row] = jnp.concatenate(totals, axis=0)


def products_call(meta, arrived, ref):
    def spec(view):
        slot = view if arrived.shape[1] == 2 else 0
        return pl.BlockSpec((1, 1, CG, 16, 128), lambda i, m: (m[2 + view], slot, 0, 0, 0))

    return pl.pallas_call(
        products,
        grid_spec=pltpu.PrefetchScalarGridSpec(
            num_scalar_prefetch=1,
            grid=(1,),
            in_specs=[
                spec(0),
                spec(1),
                pl.BlockSpec((CG, SPAN, 128), lambda i, m: (m[6], m[4], 0)),
            ],
            out_specs=pl.BlockSpec((SPAN, 16, 128), lambda i, m: (0, 0, 0)),
            scratch_shapes=[
                pltpu.VMEM((2, CG, 16, 128), jnp.float32),
                pltpu.VMEM((CG, SPAN, 128), jnp.float32),
            ],
        ),
        out_shape=pltpu.VMEM((SPAN, 16, 128), jnp.float32),
        name="products",
    )(meta, arrived, arrived, ref)


def weigh(meta, offsets, bands, taps, out):
    sub = lax.broadcasted_iota(jnp.int32, (128, D), 0)
    packed = jnp.zeros((128, D), jnp.float32)
    for view in range(2):
        packed = jnp.where(sub == view, offsets[view : view + 1, :].astype(jnp.float32), packed)
        packed = jnp.where(sub == 2 + view, bands[view : view + 1, :].astype(jnp.float32), packed)
    packed = packed.T
    lane = lax.broadcasted_iota(jnp.int32, (D, 128), 1)
    shift = jnp.bitwise_and(lane // 16 + 4 - jnp.bitwise_and(meta[6], 3), 3)
    reach = (shift + 4 * jnp.bitwise_and(lane, 7)).astype(jnp.float32)
    side = jnp.bitwise_and(lane // 8, 1)
    total = jnp.zeros((D, 128), jnp.float32)
    for view in range(2):
        offset = packed[:, view : view + 1]
        band = packed[:, 2 + view : 3 + view]
        kept = [jnp.where(band > k, taps[view, :, k : k + 1], 0.0) for k in range(4)]
        whole = kept[0] + kept[1] + kept[2] + kept[3]
        lag = jnp.where(side == view, reach, -1.0) - offset
        for k in range(4):
            total = jnp.where(lag == k, kept[k] / whole, total)
    high = total.astype(jnp.bfloat16)
    out[:, :128] = high
    out[:, 128:] = (total - high.astype(jnp.float32)).astype(jnp.bfloat16)


def weigh_call(meta, offsets, bands, taps):
    return pl.pallas_call(
        weigh,
        grid_spec=pltpu.PrefetchScalarGridSpec(
            num_scalar_prefetch=1,
            grid=(1,),
            in_specs=[
                pl.BlockSpec((2, D), lambda i, m: (0, 0)),
                pl.BlockSpec((2, D), lambda i, m: (0, 0)),
                pl.BlockSpec((2, D, 4), lambda i, m: (0, 0, 0)),
            ],
            out_specs=pl.BlockSpec((D, 256), lambda i, m: (0, 0)),
        ),
        out_shape=pltpu.VMEM((D, 256), jnp.bfloat16),
        name="weigh",
    )(meta, offsets, bands, taps)


def brink(filt, weights, pieces, right, left, stack, sums):
    lane = lax.broadcasted_iota(jnp.int32, (16, 128), 1)
    for block in range(ZL):
        ends = jnp.zeros((16, 128), jnp.float32)
        for group in range(G):
            piece = pieces[block * G + group]
            ends = jnp.where(lane == group, pltpu.roll(piece, group + 1, 1), ends)
            ends = jnp.where(lane == G + group, pltpu.roll(piece, G + group, 1), ends)
        high = ends.astype(jnp.bfloat16)
        low = (ends - high.astype(jnp.float32)).astype(jnp.bfloat16)
        for copy in range(2):
            at = 128 * copy + 16 * block
            stack[at : at + 16, :] = high
            stack[at + 64 : at + 80, :] = low
    part = jnp.dot(weights[...], stack[...], preferred_element_type=jnp.float32) * 0.125
    part = part.astype(jnp.bfloat16).astype(jnp.float32)
    slot = lax.broadcasted_iota(jnp.int32, (1, 128), 1)
    zero = jnp.zeros((8, 128), jnp.float32)
    for i in range(3):
        line = jnp.zeros((1, 128), jnp.float32)
        for group in range(G):
            line = jnp.where(slot == group, filt[group * 9 + i * 3], line)
            line = jnp.where(slot == G + group, filt[group * 9 + i * 3 + 2], line)
        sums[i, 0:8, :] = zero
        sums[i, D + 8 : D + 16, :] = zero
        sums[i, 8 : D + 8, :] = part * line
    total = (sums[0, 7 : D + 7, :] + sums[1, 8 : D + 8, :] + sums[2, 9 : D + 9, :]).T
    right[...] = jnp.sum(total[0:G], axis=0, keepdims=True)
    left[...] = jnp.sum(total[G : 2 * G], axis=0, keepdims=True)


def brink_call(filt, weights, pieces):
    edge = pltpu.VMEM((1, D), jnp.float32)
    return pl.pallas_call(
        brink,
        in_specs=[
            pl.BlockSpec(memory_space=pltpu.SMEM),
            pl.BlockSpec(memory_space=pltpu.VMEM),
            pl.BlockSpec(memory_space=pltpu.VMEM),
        ],
        out_shape=[edge, edge],
        scratch_shapes=[pltpu.VMEM((256, 128), jnp.bfloat16), pltpu.VMEM((3, D + 16, 128), jnp.float32)],
        name="brink",
    )(filt, weights, pieces)


def filtered(filt, weights, pieces, cost, stack, volume, sums):
    for group in range(G):
        lanes = slice(128 * group, 128 * group + 128)
        for block in range(ZL):
            piece = pieces[block * G + group]
            high = piece.astype(jnp.bfloat16)
            low = (piece - high.astype(jnp.float32)).astype(jnp.bfloat16)
            for copy in range(2):
                at = 128 * copy + 16 * block
                stack[at : at + 16, lanes] = high
                stack[at + 64 : at + 80, lanes] = low
    volume[...] = jnp.dot(weights[...], stack[...], preferred_element_type=jnp.float32)
    zero = jnp.zeros((8, 128), jnp.float32)
    for i in range(3):
        for j in range(3):
            sums[i, j, 0:8, :] = zero
            sums[i, j, D + 8 : D + 16, :] = zero
    step = 32

    def strip(index, carry):
        at = pl.multiple_of(index * step, step)
        totals = [[jnp.zeros((step, 128), jnp.float32) for _ in range(3)] for _ in range(3)]
        for group in range(G):
            part = volume[pl.ds(at, step), 128 * group : 128 * group + 128] * 0.125
            part = part.astype(jnp.bfloat16).astype(jnp.float32)
            for i in range(3):
                for j in range(3):
                    totals[i][j] = totals[i][j] + filt[group * 9 + i * 3 + j] * part
        for i in range(3):
            for j in range(3):
                sums[i, j, pl.ds(at + 8, step), :] = totals[i][j]
        return carry

    lax.fori_loop(0, D // step, strip, 0)
    lane = lax.broadcasted_iota(jnp.int32, (D, 128), 1)
    column = [sums[0, j, 7 : D + 7, :] + sums[1, j, 8 : D + 8, :] + sums[2, j, 9 : D + 9, :] for j in range(3)]
    before = pltpu.roll(column[0], 1, 1)
    after = pltpu.roll(column[2], 127, 1)
    cost[...] = column[1] + jnp.where(lane == 0, 0.0, before) + jnp.where(lane == 127, 0.0, after)


def filtered_call(filt, weights, pieces):
    return pl.pallas_call(
        filtered,
        in_specs=[
            pl.BlockSpec(memory_space=pltpu.SMEM),
            pl.BlockSpec(memory_space=pltpu.VMEM),
            pl.BlockSpec(memory_space=pltpu.VMEM),
        ],
        out_shape=pltpu.VMEM((D, 128), jnp.float32),
        scratch_shapes=[
            pltpu.VMEM((256, 1024), jnp.bfloat16),
            pltpu.VMEM((D, 1024), jnp.float32),
            pltpu.VMEM((3, 3, D + 16, 128), jnp.float32),
        ],
        name="filtered",
    )(filt, weights, pieces)


def expected(cost, from_left, from_right, out):
    sub = lax.broadcasted_iota(jnp.int32, (128, D), 0)
    edges = jnp.where(sub == 0, from_left[...], jnp.where(sub == 127, from_right[...], 0.0)).T
    whole = cost[...] + edges
    top = jnp.max(whole, axis=0, keepdims=True)
    grown = jnp.exp(whole - top)
    heights = lax.broadcasted_iota(jnp.int32, (D, 128), 0).astype(jnp.float32) * (1.0 / (D - 1))
    out[...] = jnp.sum(grown * heights, axis=0, keepdims=True) / jnp.sum(grown, axis=0, keepdims=True)


def expected_call(cost, from_left, from_right):
    return pl.pallas_call(
        expected,
        out_shape=jax.ShapeDtypeStruct((1, 128), jnp.float32),
        name="expected",
    )(cost, from_left, from_right)


def spread(meta, arrived, ref_feats, picks):
    windows = arrange_call(meta, arrived, picks)
    windows = lax.all_to_all(windows, ("zh", "zl"), 0, 0, tiled=True)
    return products_call(meta, near_core(windows), ref_feats).astype(jnp.float16)


def body(ref_feats, crops, owner, offsets, bands, taps, filt):
    block = lax.axis_index("zh")
    phase = lax.axis_index("zl")
    group = lax.axis_index("x") * NC + lax.axis_index("c")
    near = owner % G
    far = owner // G
    mine = jnp.where(far[1] == block * ZL + phase, near[1], near[0])
    meta = jnp.stack([near[0], near[1], far[0], far[1], block, phase, group, mine]).astype(jnp.int32)
    arrived = lax.all_to_all(crops[0], ("x", "c"), 0, 0, tiled=True)
    weights = weigh_call(meta, offsets, bands, taps)
    filt = filt.reshape(G * 9)
    meta, weights, filt = lax.optimization_barrier((meta, weights, filt))
    arrived = near_core(arrived.reshape(G, CG, 160, 128))
    pieces = lax.cond(
        jnp.logical_and(far[0] == far[1], near[0] != near[1]),
        lambda: spread(meta, arrived, ref_feats, (0, 1)),
        lambda: spread(meta, arrived, ref_feats, (7,)),
    )
    pieces = lax.all_to_all(pieces, ("zl", "x", "c"), 0, 0, tiled=True)
    pieces = pieces.astype(jnp.float32)
    weights = near_core(weights)
    pieces = near_core(pieces)
    right, left = brink_call(filt, weights, pieces)
    count = lax.axis_size("ta")
    from_left = lax.ppermute(right, "ta", [(i, i + 1) for i in range(count - 1)])
    from_right = lax.ppermute(left, "ta", [(i + 1, i) for i in range(count - 1)])
    cost = filtered_call(filt, weights, pieces)
    return expected_call(near_core(cost), near_core(from_left), near_core(from_right))


def solution(mesh):
    rows = ("zh", "zl", "x", "c")
    inner = Mesh(mesh.devices.reshape(ZH, ZL, NX, NC, mesh.shape["ta"]), rows + ("ta",))
    placed = (P(None, None, "ta"), P(rows, None, None, "ta"), P(), P(), P(), P(), P())
    return jax.shard_map(body, mesh=inner, in_specs=placed, out_specs=P(rows, "ta"), check_vma=False)
```

```python
import jax
import jax.numpy as jnp
from jax import lax
from jax.experimental import pallas as pl
from jax.experimental.pallas import tpu as pltpu
from jax.sharding import Mesh, PartitionSpec as P

G = 8
CG = 4
D = 256
ZH, ZL, NX, NC = 4, 4, 4, 2
SPAN = 32


def near_core(array):
    return pltpu.with_memory_space_constraint(array, pltpu.VMEM)


def arrange(meta, *refs):
    *sources, out, rows = refs
    for view, source in enumerate(sources):
        for chan in range(CG):
            rows[...] = source[0, chan].astype(jnp.float32)
            for block in range(ZH):
                for phase in range(ZL):
                    picked = rows[pl.ds(SPAN * block + phase, 16, stride=ZL), :]
                    out[block * ZL + phase, view, chan] = picked.astype(jnp.bfloat16)


def arrange_call(meta, arrived, picks):
    def spec(pick):
        return pl.BlockSpec((1, CG, 160, 128), lambda i, m: (m[pick], 0, 0, 0))

    shape = (16, len(picks), CG, 16, 128)
    return pl.pallas_call(
        arrange,
        grid_spec=pltpu.PrefetchScalarGridSpec(
            num_scalar_prefetch=1,
            grid=(1,),
            in_specs=[spec(pick) for pick in picks],
            out_specs=pl.BlockSpec(shape, lambda i, m: (0, 0, 0, 0, 0)),
            scratch_shapes=[pltpu.VMEM((160, 128), jnp.float32)],
        ),
        out_shape=pltpu.VMEM(shape, jnp.bfloat16),
        name="arrange",
    )(meta, *[arrived] * len(picks))


def products(meta, first, second, ref, out, rows, refs):
    phase = meta[5]
    for view, source in enumerate((first, second)):
        for chan in range(CG):
            rows[view, chan] = source[0, 0, chan].astype(jnp.float32)
    for chan in range(CG):
        refs[chan] = ref[chan].astype(jnp.float32)
    for row in range(SPAN):
        start = row // ZL + jnp.where(row % ZL > phase, 1, 0)
        totals = []
        for view in range(2):
            total = jnp.zeros((8, 128), jnp.float32)
            for chan in range(CG):
                line = refs[chan, row : row + 1, :]
                total = total + line * rows[view, chan, pl.ds(start, 8), :]
            totals.append(total)
        out[row] = jnp.concatenate(totals, axis=0)


def products_call(meta, arrived, ref):
    def spec(view):
        slot = view if arrived.shape[1] == 2 else 0
        return pl.BlockSpec((1, 1, CG, 16, 128), lambda i, m: (m[2 + view], slot, 0, 0, 0))

    return pl.pallas_call(
        products,
        grid_spec=pltpu.PrefetchScalarGridSpec(
            num_scalar_prefetch=1,
            grid=(1,),
            in_specs=[
                spec(0),
                spec(1),
                pl.BlockSpec((CG, SPAN, 128), lambda i, m: (m[6], m[4], 0)),
            ],
            out_specs=pl.BlockSpec((SPAN, 16, 128), lambda i, m: (0, 0, 0)),
            scratch_shapes=[
                pltpu.VMEM((2, CG, 16, 128), jnp.float32),
                pltpu.VMEM((CG, SPAN, 128), jnp.float32),
            ],
        ),
        out_shape=pltpu.VMEM((SPAN, 16, 128), jnp.float32),
        name="products",
    )(meta, arrived, arrived, ref)


def weigh(meta, filt, offsets, bands, taps, out, lines):
    slot = lax.broadcasted_iota(jnp.int32, (8, 128), 1)
    lag = lax.broadcasted_iota(jnp.int32, (8, 128), 0)
    rows = jnp.zeros((8, 128), jnp.float32)
    for i in range(3):
        for group in range(G):
            rows = jnp.where((lag == i) & (slot == group), filt[group * 9 + i * 3], rows)
            rows = jnp.where((lag == i) & (slot == G + group), filt[group * 9 + i * 3 + 2], rows)
    lines[...] = rows
    sub = lax.broadcasted_iota(jnp.int32, (128, D), 0)
    packed = jnp.zeros((128, D), jnp.float32)
    for view in range(2):
        packed = jnp.where(sub == view, offsets[view : view + 1, :].astype(jnp.float32), packed)
        packed = jnp.where(sub == 2 + view, bands[view : view + 1, :].astype(jnp.float32), packed)
    packed = packed.T
    lane = lax.broadcasted_iota(jnp.int32, (D, 128), 1)
    shift = jnp.bitwise_and(lane // 16 + 4 - jnp.bitwise_and(meta[6], 3), 3)
    reach = (shift + 4 * jnp.bitwise_and(lane, 7)).astype(jnp.float32)
    side = jnp.bitwise_and(lane // 8, 1)
    total = jnp.zeros((D, 128), jnp.float32)
    for view in range(2):
        offset = packed[:, view : view + 1]
        band = packed[:, 2 + view : 3 + view]
        kept = [jnp.where(band > k, taps[view, :, k : k + 1], 0.0) for k in range(4)]
        whole = kept[0] + kept[1] + kept[2] + kept[3]
        lag = jnp.where(side == view, reach, -1.0) - offset
        for k in range(4):
            total = jnp.where(lag == k, kept[k] / whole, total)
    high = total.astype(jnp.bfloat16)
    out[:, :128] = high
    out[:, 128:] = (total - high.astype(jnp.float32)).astype(jnp.bfloat16)


def weigh_call(meta, filt, offsets, bands, taps):
    return pl.pallas_call(
        weigh,
        grid_spec=pltpu.PrefetchScalarGridSpec(
            num_scalar_prefetch=2,
            grid=(1,),
            in_specs=[
                pl.BlockSpec((2, D), lambda i, m, f: (0, 0)),
                pl.BlockSpec((2, D), lambda i, m, f: (0, 0)),
                pl.BlockSpec((2, D, 4), lambda i, m, f: (0, 0, 0)),
            ],
            out_specs=[pl.BlockSpec((D, 256), lambda i, m, f: (0, 0)), pl.BlockSpec((8, 128), lambda i, m, f: (0, 0))],
        ),
        out_shape=[pltpu.VMEM((D, 256), jnp.bfloat16), pltpu.VMEM((8, 128), jnp.float32)],
        name="weigh",
    )(meta, filt, offsets, bands, taps)


def brink(lines, weights, pieces, right, left, stack, sums):
    lane = lax.broadcasted_iota(jnp.int32, (16, 128), 1)
    for block in range(ZL):
        ends = jnp.zeros((16, 128), jnp.float32)
        for group in range(G):
            piece = pieces[block * G + group]
            ends = jnp.where(lane == group, pltpu.roll(piece, group + 1, 1), ends)
            ends = jnp.where(lane == G + group, pltpu.roll(piece, G + group, 1), ends)
        high = ends.astype(jnp.bfloat16)
        low = (ends - high.astype(jnp.float32)).astype(jnp.bfloat16)
        for copy in range(2):
            at = 128 * copy + 16 * block
            stack[at : at + 16, :] = high
            stack[at + 64 : at + 80, :] = low
    part = jnp.dot(weights[...], stack[...], preferred_element_type=jnp.float32) * 0.125
    part = part.astype(jnp.bfloat16).astype(jnp.float32)
    zero = jnp.zeros((8, 128), jnp.float32)
    for i in range(3):
        line = lines[i : i + 1, :]
        sums[i, 0:8, :] = zero
        sums[i, D + 8 : D + 16, :] = zero
        sums[i, 8 : D + 8, :] = part * line
    total = (sums[0, 7 : D + 7, :] + sums[1, 8 : D + 8, :] + sums[2, 9 : D + 9, :]).T
    right[...] = jnp.sum(total[0:G], axis=0, keepdims=True)
    left[...] = jnp.sum(total[G : 2 * G], axis=0, keepdims=True)


def brink_call(lines, weights, pieces):
    edge = pltpu.VMEM((1, D), jnp.float32)
    return pl.pallas_call(
        brink,
        in_specs=[
            pl.BlockSpec(memory_space=pltpu.VMEM),
            pl.BlockSpec(memory_space=pltpu.VMEM),
            pl.BlockSpec(memory_space=pltpu.VMEM),
        ],
        out_shape=[edge, edge],
        scratch_shapes=[pltpu.VMEM((256, 128), jnp.bfloat16), pltpu.VMEM((3, D + 16, 128), jnp.float32)],
        name="brink",
    )(lines, weights, pieces)


def filtered(filt, weights, pieces, cost, stack, volume, sums):
    for group in range(G):
        lanes = slice(128 * group, 128 * group + 128)
        for block in range(ZL):
            piece = pieces[block * G + group]
            high = piece.astype(jnp.bfloat16)
            low = (piece - high.astype(jnp.float32)).astype(jnp.bfloat16)
            for copy in range(2):
                at = 128 * copy + 16 * block
                stack[at : at + 16, lanes] = high
                stack[at + 64 : at + 80, lanes] = low
    volume[...] = jnp.dot(weights[...], stack[...], preferred_element_type=jnp.float32)
    zero = jnp.zeros((8, 128), jnp.float32)
    for i in range(3):
        for j in range(3):
            sums[i, j, 0:8, :] = zero
            sums[i, j, D + 8 : D + 16, :] = zero
    step = 32

    def strip(index, carry):
        at = pl.multiple_of(index * step, step)
        totals = [[jnp.zeros((step, 128), jnp.float32) for _ in range(3)] for _ in range(3)]
        for group in range(G):
            part = volume[pl.ds(at, step), 128 * group : 128 * group + 128] * 0.125
            part = part.astype(jnp.bfloat16).astype(jnp.float32)
            for i in range(3):
                for j in range(3):
                    totals[i][j] = totals[i][j] + filt[group * 9 + i * 3 + j] * part
        for i in range(3):
            for j in range(3):
                sums[i, j, pl.ds(at + 8, step), :] = totals[i][j]
        return carry

    lax.fori_loop(0, D // step, strip, 0)
    lane = lax.broadcasted_iota(jnp.int32, (D, 128), 1)
    column = [sums[0, j, 7 : D + 7, :] + sums[1, j, 8 : D + 8, :] + sums[2, j, 9 : D + 9, :] for j in range(3)]
    before = pltpu.roll(column[0], 1, 1)
    after = pltpu.roll(column[2], 127, 1)
    cost[...] = column[1] + jnp.where(lane == 0, 0.0, before) + jnp.where(lane == 127, 0.0, after)


def filtered_call(filt, weights, pieces):
    return pl.pallas_call(
        filtered,
        in_specs=[
            pl.BlockSpec(memory_space=pltpu.SMEM),
            pl.BlockSpec(memory_space=pltpu.VMEM),
            pl.BlockSpec(memory_space=pltpu.VMEM),
        ],
        out_shape=pltpu.VMEM((D, 128), jnp.float32),
        scratch_shapes=[
            pltpu.VMEM((256, 1024), jnp.bfloat16),
            pltpu.VMEM((D, 1024), jnp.float32),
            pltpu.VMEM((3, 3, D + 16, 128), jnp.float32),
        ],
        name="filtered",
    )(filt, weights, pieces)


def expected(cost, from_left, from_right, out):
    sub = lax.broadcasted_iota(jnp.int32, (128, D), 0)
    edges = jnp.where(sub == 0, from_left[...], jnp.where(sub == 127, from_right[...], 0.0)).T
    whole = cost[...] + edges
    top = jnp.max(whole, axis=0, keepdims=True)
    grown = jnp.exp(whole - top)
    heights = lax.broadcasted_iota(jnp.int32, (D, 128), 0).astype(jnp.float32) * (1.0 / (D - 1))
    out[...] = jnp.sum(grown * heights, axis=0, keepdims=True) / jnp.sum(grown, axis=0, keepdims=True)


def expected_call(cost, from_left, from_right):
    return pl.pallas_call(
        expected,
        out_shape=jax.ShapeDtypeStruct((1, 128), jnp.float32),
        name="expected",
    )(cost, from_left, from_right)


def spread(meta, arrived, ref_feats, picks):
    windows = arrange_call(meta, arrived, picks)
    windows = lax.all_to_all(windows, ("zh", "zl"), 0, 0, tiled=True)
    return products_call(meta, near_core(windows), ref_feats).astype(jnp.float16)


def body(ref_feats, crops, owner, offsets, bands, taps, filt):
    block = lax.axis_index("zh")
    phase = lax.axis_index("zl")
    group = lax.axis_index("x") * NC + lax.axis_index("c")
    near = owner % G
    far = owner // G
    mine = jnp.where(far[1] == block * ZL + phase, near[1], near[0])
    meta = jnp.stack([near[0], near[1], far[0], far[1], block, phase, group, mine]).astype(jnp.int32)
    arrived = lax.all_to_all(crops[0], ("x", "c"), 0, 0, tiled=True)
    filt = filt.reshape(G * 9)
    weights, lines = weigh_call(meta, filt, offsets, bands, taps)
    meta, weights, lines, filt = lax.optimization_barrier((meta, weights, lines, filt))
    arrived = near_core(arrived.reshape(G, CG, 160, 128))
    pieces = lax.cond(
        jnp.logical_and(far[0] == far[1], near[0] != near[1]),
        lambda: spread(meta, arrived, ref_feats, (0, 1)),
        lambda: spread(meta, arrived, ref_feats, (7,)),
    )
    pieces = lax.all_to_all(pieces, ("zl", "x", "c"), 0, 0, tiled=True)
    pieces = pieces.astype(jnp.float32)
    weights = near_core(weights)
    pieces = near_core(pieces)
    right, left = brink_call(near_core(lines), weights, pieces)
    count = lax.axis_size("ta")
    from_left = lax.ppermute(right, "ta", [(i, i + 1) for i in range(count - 1)])
    from_right = lax.ppermute(left, "ta", [(i + 1, i) for i in range(count - 1)])
    cost = filtered_call(filt, weights, pieces)
    return expected_call(near_core(cost), near_core(from_left), near_core(from_right))


def solution(mesh):
    rows = ("zh", "zl", "x", "c")
    inner = Mesh(mesh.devices.reshape(ZH, ZL, NX, NC, mesh.shape["ta"]), rows + ("ta",))
    placed = (P(None, None, "ta"), P(rows, None, None, "ta"), P(), P(), P(), P(), P())
    return jax.shard_map(body, mesh=inner, in_specs=placed, out_specs=P(rows, "ta"), check_vma=False)
```

```python
import jax
import jax.numpy as jnp
from jax import lax
from jax.experimental import pallas as pl
from jax.experimental.pallas import tpu as pltpu
from jax.sharding import Mesh, PartitionSpec as P

G = 8
CG = 4
D = 256
ZH, ZL, NX, NC = 4, 4, 4, 2
SPAN = 32


def near_core(array):
    return pltpu.with_memory_space_constraint(array, pltpu.VMEM)


def arrange(meta, *refs):
    *sources, out, rows = refs
    for view, source in enumerate(sources):
        for chan in range(CG):
            rows[...] = source[0, chan].astype(jnp.float32)
            for block in range(ZH):
                for phase in range(ZL):
                    picked = rows[pl.ds(SPAN * block + phase, 16, stride=ZL), :]
                    out[block * ZL + phase, view, chan] = picked.astype(jnp.bfloat16)


def arrange_call(meta, arrived, picks):
    def spec(pick):
        return pl.BlockSpec((1, CG, 160, 128), lambda i, m: (m[pick], 0, 0, 0))

    shape = (16, len(picks), CG, 16, 128)
    return pl.pallas_call(
        arrange,
        grid_spec=pltpu.PrefetchScalarGridSpec(
            num_scalar_prefetch=1,
            grid=(1,),
            in_specs=[spec(pick) for pick in picks],
            out_specs=pl.BlockSpec(shape, lambda i, m: (0, 0, 0, 0, 0)),
            scratch_shapes=[pltpu.VMEM((160, 128), jnp.float32)],
        ),
        out_shape=pltpu.VMEM(shape, jnp.bfloat16),
        name="arrange",
    )(meta, *[arrived] * len(picks))


def products(meta, first, second, ref, out, rows, refs):
    phase = meta[5]
    for view, source in enumerate((first, second)):
        for chan in range(CG):
            rows[view, chan] = source[0, 0, chan].astype(jnp.float32)
    for chan in range(CG):
        refs[chan] = ref[chan].astype(jnp.float32)
    for row in range(SPAN):
        start = row // ZL + jnp.where(row % ZL > phase, 1, 0)
        totals = []
        for view in range(2):
            total = jnp.zeros((8, 128), jnp.float32)
            for chan in range(CG):
                line = refs[chan, row : row + 1, :]
                total = total + line * rows[view, chan, pl.ds(start, 8), :]
            totals.append(total)
        out[row] = jnp.concatenate(totals, axis=0)


def products_call(meta, arrived, ref):
    def spec(view):
        slot = view if arrived.shape[1] == 2 else 0
        return pl.BlockSpec((1, 1, CG, 16, 128), lambda i, m: (m[2 + view], slot, 0, 0, 0))

    return pl.pallas_call(
        products,
        grid_spec=pltpu.PrefetchScalarGridSpec(
            num_scalar_prefetch=1,
            grid=(1,),
            in_specs=[
                spec(0),
                spec(1),
                pl.BlockSpec((CG, SPAN, 128), lambda i, m: (m[6], m[4], 0)),
            ],
            out_specs=pl.BlockSpec((SPAN, 16, 128), lambda i, m: (0, 0, 0)),
            scratch_shapes=[
                pltpu.VMEM((2, CG, 16, 128), jnp.float32),
                pltpu.VMEM((CG, SPAN, 128), jnp.float32),
            ],
        ),
        out_shape=pltpu.VMEM((SPAN, 16, 128), jnp.float32),
        name="products",
    )(meta, arrived, arrived, ref)


def weigh(meta, filt, offsets, bands, taps, out, lines):
    slot = lax.broadcasted_iota(jnp.int32, (8, 128), 1)
    lag = lax.broadcasted_iota(jnp.int32, (8, 128), 0)
    rows = jnp.zeros((8, 128), jnp.float32)
    for i in range(3):
        for group in range(G):
            rows = jnp.where((lag == i) & (slot == group), filt[group * 9 + i * 3], rows)
            rows = jnp.where((lag == i) & (slot == G + group), filt[group * 9 + i * 3 + 2], rows)
    even = jnp.where(jnp.bitwise_and(meta[8], 1) == 0, 1.0, 0.0)
    lines[...] = jnp.where(lag == 3, even, rows)
    sub = lax.broadcasted_iota(jnp.int32, (128, D), 0)
    packed = jnp.zeros((128, D), jnp.float32)
    for view in range(2):
        packed = jnp.where(sub == view, offsets[view : view + 1, :].astype(jnp.float32), packed)
        packed = jnp.where(sub == 2 + view, bands[view : view + 1, :].astype(jnp.float32), packed)
    packed = packed.T
    lane = lax.broadcasted_iota(jnp.int32, (D, 128), 1)
    shift = jnp.bitwise_and(lane // 16 + 4 - jnp.bitwise_and(meta[6], 3), 3)
    reach = (shift + 4 * jnp.bitwise_and(lane, 7)).astype(jnp.float32)
    side = jnp.bitwise_and(lane // 8, 1)
    total = jnp.zeros((D, 128), jnp.float32)
    for view in range(2):
        offset = packed[:, view : view + 1]
        band = packed[:, 2 + view : 3 + view]
        kept = [jnp.where(band > k, taps[view, :, k : k + 1], 0.0) for k in range(4)]
        whole = kept[0] + kept[1] + kept[2] + kept[3]
        lag = jnp.where(side == view, reach, -1.0) - offset
        for k in range(4):
            total = jnp.where(lag == k, kept[k] / whole, total)
    high = total.astype(jnp.bfloat16)
    out[:, :128] = high
    out[:, 128:] = (total - high.astype(jnp.float32)).astype(jnp.bfloat16)


def weigh_call(meta, filt, offsets, bands, taps):
    return pl.pallas_call(
        weigh,
        grid_spec=pltpu.PrefetchScalarGridSpec(
            num_scalar_prefetch=2,
            grid=(1,),
            in_specs=[
                pl.BlockSpec((2, D), lambda i, m, f: (0, 0)),
                pl.BlockSpec((2, D), lambda i, m, f: (0, 0)),
                pl.BlockSpec((2, D, 4), lambda i, m, f: (0, 0, 0)),
            ],
            out_specs=[pl.BlockSpec((D, 256), lambda i, m, f: (0, 0)), pl.BlockSpec((8, 128), lambda i, m, f: (0, 0))],
        ),
        out_shape=[pltpu.VMEM((D, 256), jnp.bfloat16), pltpu.VMEM((8, 128), jnp.float32)],
        name="weigh",
    )(meta, filt, offsets, bands, taps)


def brink(lines, weights, pieces, right, left, stack, sums):
    lane = lax.broadcasted_iota(jnp.int32, (16, 128), 1)
    for block in range(ZL):
        ends = jnp.zeros((16, 128), jnp.float32)
        for group in range(G):
            piece = pieces[block * G + group]
            ends = jnp.where(lane == group, pltpu.roll(piece, group + 1, 1), ends)
            ends = jnp.where(lane == G + group, pltpu.roll(piece, G + group, 1), ends)
        high = ends.astype(jnp.bfloat16)
        low = (ends - high.astype(jnp.float32)).astype(jnp.bfloat16)
        for copy in range(2):
            at = 128 * copy + 16 * block
            stack[at : at + 16, :] = high
            stack[at + 64 : at + 80, :] = low
    part = jnp.dot(weights[...], stack[...], preferred_element_type=jnp.float32) * 0.125
    part = part.astype(jnp.bfloat16).astype(jnp.float32)
    zero = jnp.zeros((8, 128), jnp.float32)
    for i in range(3):
        line = lines[i : i + 1, :]
        sums[i, 0:8, :] = zero
        sums[i, D + 8 : D + 16, :] = zero
        sums[i, 8 : D + 8, :] = part * line
    total = (sums[0, 7 : D + 7, :] + sums[1, 8 : D + 8, :] + sums[2, 9 : D + 9, :]).T
    onward = jnp.sum(total[0:G], axis=0, keepdims=True)
    back = jnp.sum(total[G : 2 * G], axis=0, keepdims=True)
    even = jnp.concatenate([lines[3:4, :], lines[3:4, :]], axis=1) > 0.5
    right[...] = jnp.where(even, onward, back)
    left[...] = jnp.where(even, back, onward)


def brink_call(lines, weights, pieces):
    edge = pltpu.VMEM((1, D), jnp.float32)
    return pl.pallas_call(
        brink,
        in_specs=[
            pl.BlockSpec(memory_space=pltpu.VMEM),
            pl.BlockSpec(memory_space=pltpu.VMEM),
            pl.BlockSpec(memory_space=pltpu.VMEM),
        ],
        out_shape=[edge, edge],
        scratch_shapes=[pltpu.VMEM((256, 128), jnp.bfloat16), pltpu.VMEM((3, D + 16, 128), jnp.float32)],
        name="brink",
    )(lines, weights, pieces)


def filtered(filt, weights, pieces, cost, stack, volume, sums):
    for group in range(G):
        lanes = slice(128 * group, 128 * group + 128)
        for block in range(ZL):
            piece = pieces[block * G + group]
            high = piece.astype(jnp.bfloat16)
            low = (piece - high.astype(jnp.float32)).astype(jnp.bfloat16)
            for copy in range(2):
                at = 128 * copy + 16 * block
                stack[at : at + 16, lanes] = high
                stack[at + 64 : at + 80, lanes] = low
    volume[...] = jnp.dot(weights[...], stack[...], preferred_element_type=jnp.float32)
    zero = jnp.zeros((8, 128), jnp.float32)
    for i in range(3):
        for j in range(3):
            sums[i, j, 0:8, :] = zero
            sums[i, j, D + 8 : D + 16, :] = zero
    step = 32

    def strip(index, carry):
        at = pl.multiple_of(index * step, step)
        totals = [[jnp.zeros((step, 128), jnp.float32) for _ in range(3)] for _ in range(3)]
        for group in range(G):
            part = volume[pl.ds(at, step), 128 * group : 128 * group + 128] * 0.125
            part = part.astype(jnp.bfloat16).astype(jnp.float32)
            for i in range(3):
                for j in range(3):
                    totals[i][j] = totals[i][j] + filt[group * 9 + i * 3 + j] * part
        for i in range(3):
            for j in range(3):
                sums[i, j, pl.ds(at + 8, step), :] = totals[i][j]
        return carry

    lax.fori_loop(0, D // step, strip, 0)
    lane = lax.broadcasted_iota(jnp.int32, (D, 128), 1)
    column = [sums[0, j, 7 : D + 7, :] + sums[1, j, 8 : D + 8, :] + sums[2, j, 9 : D + 9, :] for j in range(3)]
    before = pltpu.roll(column[0], 1, 1)
    after = pltpu.roll(column[2], 127, 1)
    cost[...] = column[1] + jnp.where(lane == 0, 0.0, before) + jnp.where(lane == 127, 0.0, after)


def filtered_call(filt, weights, pieces):
    return pl.pallas_call(
        filtered,
        in_specs=[
            pl.BlockSpec(memory_space=pltpu.SMEM),
            pl.BlockSpec(memory_space=pltpu.VMEM),
            pl.BlockSpec(memory_space=pltpu.VMEM),
        ],
        out_shape=pltpu.VMEM((D, 128), jnp.float32),
        scratch_shapes=[
            pltpu.VMEM((256, 1024), jnp.bfloat16),
            pltpu.VMEM((D, 1024), jnp.float32),
            pltpu.VMEM((3, 3, D + 16, 128), jnp.float32),
        ],
        name="filtered",
    )(filt, weights, pieces)


def expected(cost, lines, pair, cross, out):
    sub = lax.broadcasted_iota(jnp.int32, (128, D), 0)
    even = jnp.concatenate([lines[3:4, :], lines[3:4, :]], axis=1) > 0.5
    from_left = jnp.where(even, cross[...], pair[...])
    from_right = jnp.where(even, pair[...], cross[...])
    edges = jnp.where(sub == 0, from_left, jnp.where(sub == 127, from_right, 0.0)).T
    whole = cost[...] + edges
    top = jnp.max(whole, axis=0, keepdims=True)
    grown = jnp.exp(whole - top)
    heights = lax.broadcasted_iota(jnp.int32, (D, 128), 0).astype(jnp.float32) * (1.0 / (D - 1))
    out[...] = jnp.sum(grown * heights, axis=0, keepdims=True) / jnp.sum(grown, axis=0, keepdims=True)


def expected_call(cost, lines, pair, cross):
    return pl.pallas_call(
        expected,
        out_shape=jax.ShapeDtypeStruct((1, 128), jnp.float32),
        name="expected",
    )(cost, lines, pair, cross)


def spread(meta, arrived, ref_feats, picks):
    windows = arrange_call(meta, arrived, picks)
    windows = lax.all_to_all(windows, ("zh", "zl"), 0, 0, tiled=True)
    return products_call(meta, near_core(windows), ref_feats).astype(jnp.float16)


def body(ref_feats, crops, owner, offsets, bands, taps, filt):
    block = lax.axis_index("zh")
    phase = lax.axis_index("zl")
    group = lax.axis_index("x") * NC + lax.axis_index("c")
    near = owner % G
    far = owner // G
    mine = jnp.where(far[1] == block * ZL + phase, near[1], near[0])
    meta = jnp.stack([near[0], near[1], far[0], far[1], block, phase, group, mine, lax.axis_index("ta")]).astype(jnp.int32)
    arrived = lax.all_to_all(crops[0], ("x", "c"), 0, 0, tiled=True)
    filt = filt.reshape(G * 9)
    weights, lines = weigh_call(meta, filt, offsets, bands, taps)
    meta, weights, lines, filt = lax.optimization_barrier((meta, weights, lines, filt))
    arrived = near_core(arrived.reshape(G, CG, 160, 128))
    pieces = lax.cond(
        jnp.logical_and(far[0] == far[1], near[0] != near[1]),
        lambda: spread(meta, arrived, ref_feats, (0, 1)),
        lambda: spread(meta, arrived, ref_feats, (7,)),
    )
    pieces = lax.all_to_all(pieces, ("zl", "x", "c"), 0, 0, tiled=True)
    pieces = pieces.astype(jnp.float32)
    weights = near_core(weights)
    pieces = near_core(pieces)
    right, left = brink_call(near_core(lines), weights, pieces)
    count = lax.axis_size("ta")
    pair = lax.ppermute(right, "ta", [(i, i ^ 1) for i in range(count) if i ^ 1 < count])
    cross = lax.ppermute(left, "ta", [p for i in range(1, count - 1, 2) for p in ((i, i + 1), (i + 1, i))])
    cost = filtered_call(filt, weights, pieces)
    return expected_call(near_core(cost), near_core(lines), near_core(pair), near_core(cross))


def solution(mesh):
    rows = ("zh", "zl", "x", "c")
    inner = Mesh(mesh.devices.reshape(ZH, ZL, NX, NC, mesh.shape["ta"]), rows + ("ta",))
    placed = (P(None, None, "ta"), P(rows, None, None, "ta"), P(), P(), P(), P(), P())
    return jax.shard_map(body, mesh=inner, in_specs=placed, out_specs=P(rows, "ta"), check_vma=False)
```
